256 devices in a mesh: ctx: 64 (over y, z, core), head: 4 (over x).
Axes of the slice: x: 4, y: 4, z: 8, core: 2. Of those that a mesh axis runs over, the one named last changes fastest.
Arguments:
- q_lin: bfloat16 [8192, 8192], P('ctx', 'head'), may hold values from -6 to 6
- k_lin: bfloat16 [8192, 8192], P('ctx', 'head'), may hold values from -6 to 6
- v_lin: bfloat16 [8192, 8192], P('ctx', 'head'), may hold values from -70 to 70
- log_decay: float32 [64, 8192], P('head', 'ctx'), may hold values from -1 to 0
- gate: bfloat16 [8192, 8192], P('ctx', 'head'), may hold values from -6 to 6
- norm_gain: float32 [8192], P('head'), may hold values from 0.1 to 1.9
- queries: bfloat16 [8192, 8192], P('ctx', 'head'), may hold values from -8 to 8
- keys: bfloat16 [8192, 1024], P('ctx', 'head'), may hold values from -4 to 4
- values: bfloat16 [8192, 1024], P('ctx', 'head'), may hold values from -6 to 6
- order: int32 [64], P('ctx'), may hold values from 0 to 63, each once
Outputs:
- mixed: bfloat16 [8192, 8192], P('ctx', 'head')
- attended: bfloat16 [8192, 8192], P('ctx', 'head')
The draws below stay inside these ranges and needn't reach their ends.
Inputs may be any that keep to these rules, and one draw needn't show every extreme that they name: order is a permutation of the 64 sequence shards.
All inputs are finite; a program needn't handle non-finite values.
Results may differ from the reference program's by a relative error of at most 0.0045.
Values may be sent and summed in bfloat16 or wider, within the bound.
A program may use at most 128 MiB of HBM per device.

```python
import math
import jax
import jax.numpy as jnp
from jax import lax

H = 64
HD = 128
KVH = 8
TOK_DEV = 128
BLOCK = 128
SEQ = 8192
N_CTX = 64


def draw_log_decay(key, part):
    parts = jax.random.split(key, 7)
    rank = jax.random.permutation(parts[0], H)
    kind = rank % 4
    fast = kind == 0
    medium = kind == 1
    fast_rate = jnp.exp(jax.random.uniform(parts[1], (H,), jnp.float32, math.log(1.0 / 50.0), math.log(1.0 / 30.0)))
    medium_rate = jnp.exp(jax.random.uniform(parts[6], (H,), jnp.float32, math.log(1.0 / TOK_DEV), math.log(3.0 / TOK_DEV)))
    slow_rate = jnp.exp(jax.random.uniform(parts[2], (H,), jnp.float32, math.log(0.05 * math.log(10.0) / SEQ), math.log(0.35 * math.log(10.0) / SEQ)))
    rate = jnp.where(fast, fast_rate, jnp.where(medium, medium_rate, slow_rate))
    factor = jnp.exp(jax.random.uniform(parts[3], (H, SEQ), jnp.float32, math.log(0.5), math.log(2.0)))
    values = -rate[:, None] * factor
    spots = jax.random.randint(parts[4], (H, 2), 0, SEQ)
    keep = jax.random.uniform(parts[5], (H, 2), jnp.float32, 0.5, 0.8)
    hit = lax.iota(jnp.int32, SEQ)[None, None, :] == spots[:, :, None]
    values = values + jnp.sum(jnp.where(hit, jnp.log(keep)[:, :, None], 0.0), axis=1)
    values = jnp.maximum(values, -1.0)
    return values.astype(jnp.float32)


def draw_v_lin(key, part):
    parts = jax.random.split(key, 3)
    width = H * HD
    base = jnp.clip(jax.random.normal(parts[0], (SEQ, width), jnp.float32), -4.0, 4.0)
    column = jnp.exp(jax.random.uniform(parts[1], (width,), jnp.float32, 0.0, math.log(10.0))) / math.sqrt(10.0)
    rising = jnp.exp(math.log(3.0) * lax.iota(jnp.float32, width) / (width - 1)) / math.sqrt(3.0)
    row = jnp.exp(jax.random.uniform(parts[2], (SEQ,), jnp.float32, 0.0, math.log(10.0))) / math.sqrt(10.0)
    return (base * (column * rising)[None, :] * row[:, None]).astype(jnp.bfloat16)


def draw_queries(key, part):
    base_key = jax.random.fold_in(key, 11)
    base = jnp.clip(jax.random.normal(base_key, (SEQ, H, HD), jnp.float32), -4.0, 4.0)
    return base.reshape(SEQ, H * HD).astype(jnp.bfloat16)


def draw_keys(key, part):
    base_key = jax.random.fold_in(key, 13)
    base = jnp.clip(jax.random.normal(base_key, (SEQ, KVH, HD), jnp.float32), -4.0, 4.0)
    return base.reshape(SEQ, KVH * HD).astype(jnp.bfloat16)


def block_levels(rng, dims, shards, least, top_value):
    factor_of = 1.0
    for axis_at, blocks in shards:
        steps = jax.random.uniform(jax.random.fold_in(jax.random.fold_in(rng, 6), axis_at), (blocks,), jnp.float32, least / len(shards), top_value / len(shards))
        factor_of = factor_of * jnp.repeat(jnp.exp(steps), dims[axis_at] // blocks).reshape((-1,) + (1,) * (len(dims) - 1 - axis_at))
    return factor_of


def bell_draw(stream_key, shape, deviation, bound, shards=(), kind=jnp.bfloat16):
    gain = block_levels(stream_key, shape, shards, -0.22, 0.18) if shards else 1.0
    drawn = jax.random.normal(stream_key, shape, jnp.float32) * deviation * gain
    return jnp.minimum(jnp.maximum(drawn, -bound), bound).astype(kind)


def setup_inputs(seed: int = 0) -> dict:
    arg_keys = jax.random.split(jax.random.key(seed), 11)
    q_lin = bell_draw(arg_keys[0], (SEQ, H * HD), 1.0, 6.0, ((0, 64), (1, 4)))
    k_lin = bell_draw(arg_keys[1], (SEQ, H * HD), 1.0, 6.0, ((0, 64), (1, 4)))
    v_lin = draw_v_lin(jax.random.fold_in(arg_keys[10], 71), 0)
    log_decay = draw_log_decay(jax.random.fold_in(arg_keys[10], 71), 0)
    gate = bell_draw(arg_keys[4], (SEQ, H * HD), 1.5, 6.0, ((0, 64), (1, 4)))
    norm_gain = jnp.clip(1.0 + 0.18 * jax.random.normal(arg_keys[5], (H * HD,), jnp.float32), 0.1, 1.9)
    queries = draw_queries(jax.random.fold_in(arg_keys[10], 71), 0)
    keys = draw_keys(jax.random.fold_in(arg_keys[10], 71), 0)
    values = bell_draw(arg_keys[8], (SEQ, KVH * HD), 1.0, 6.0, ((0, 64), (1, 4)))
    order = jax.random.permutation(arg_keys[9], N_CTX).astype(jnp.int32)
    return {"q_lin": q_lin, "k_lin": k_lin, "v_lin": v_lin, "log_decay": log_decay, "gate": gate, "norm_gain": norm_gain, "queries": queries, "keys": keys, "values": values, "order": order}


EPS = 1e-06
HIGH = lax.Precision.HIGHEST

def lightning_blocks(qa, ka, va, decay_log, state0):
    total = qa.shape[0]
    heads = qa.shape[1]
    count = total // BLOCK
    qb_all = qa.reshape(count, BLOCK, heads, HD)
    kb_all = ka.reshape(count, BLOCK, heads, HD)
    vb_all = va.reshape(count, BLOCK, heads, HD)
    gb_all = decay_log.reshape(heads, count, BLOCK).transpose(1, 0, 2)

    def step(state, pieces):
        qb, kb, vb, gb = pieces
        cum = jnp.cumsum(gb, axis=1)
        scores = jnp.einsum('thd,shd->hts', qb.astype(jnp.float32), kb.astype(jnp.float32), precision=HIGH)
        lower = lax.iota(jnp.int32, BLOCK)[:, None] >= lax.iota(jnp.int32, BLOCK)[None, :]
        diff = cum[:, :, None] - cum[:, None, :]
        decay = jnp.where(lower[None], jnp.exp(jnp.where(lower[None], diff, 0.0)), 0.0)
        weights = (scores * decay).astype(jnp.bfloat16)
        intra = jnp.einsum('hts,shd->thd', weights.astype(jnp.float32), vb.astype(jnp.float32), precision=HIGH)
        qdec = qb.astype(jnp.float32) * jnp.exp(cum).T[:, :, None]
        inter = jnp.einsum('thd,hde->the', qdec, state, precision=HIGH)
        kdec = kb.astype(jnp.float32) * jnp.exp(cum[:, -1:] - cum).T[:, :, None]
        update = jnp.einsum('thd,the->hde', kdec, vb.astype(jnp.float32), precision=HIGH)
        state_new = jnp.exp(cum[:, -1])[:, None, None] * state + update
        return (state_new, intra + inter)
    state, outs = lax.scan(step, state0, (qb_all, kb_all, vb_all, gb_all))
    return (outs.reshape(total, heads, HD), state)

def reference(q_lin, k_lin, v_lin, log_decay, gate, norm_gain, queries, keys, values, order):
    qa = jax.nn.silu(q_lin.astype(jnp.float32)).astype(jnp.bfloat16).reshape(SEQ, H, HD)
    ka = jax.nn.silu(k_lin.astype(jnp.float32)).astype(jnp.bfloat16).reshape(SEQ, H, HD)
    va = jax.nn.silu(v_lin.astype(jnp.float32)).astype(jnp.bfloat16).reshape(SEQ, H, HD)
    state0 = jnp.zeros((H, HD, HD), jnp.float32)
    lin, state_end = lightning_blocks(qa, ka, va, log_decay, state0)
    squares = lax.optimization_barrier(jnp.sum(lin * lin, axis=(1, 2)))
    inv = lax.rsqrt(squares / (H * HD) + EPS)
    gated = jax.nn.sigmoid(gate.astype(jnp.float32).reshape(SEQ, H, HD))
    mixed = (lin * inv[:, None, None] * norm_gain.reshape(H, HD) * gated).astype(jnp.bfloat16).reshape(SEQ, H * HD)
    group = H // KVH
    keys_f = keys.astype(jnp.float32).reshape(SEQ, KVH, HD)
    values_f = values.astype(jnp.float32).reshape(SEQ, KVH, HD)
    kpos = lax.iota(jnp.int32, SEQ)
    scale = 1.0 / math.sqrt(HD)

    def shard(index):
        rows = lax.dynamic_slice_in_dim(queries, (index * TOK_DEV).astype(jnp.int32), TOK_DEV, 0)
        qg = rows.astype(jnp.float32).reshape(TOK_DEV, KVH, group, HD)
        qpos = order[index] * TOK_DEV + lax.iota(jnp.int32, TOK_DEV)
        scores = jnp.einsum('tkgd,skd->kgts', qg, keys_f, precision=HIGH) * scale
        mask = kpos[None, :] <= qpos[:, None]
        masked = jnp.where(mask, scores, -1e+30)
        top = lax.optimization_barrier(jnp.max(masked, axis=-1))
        probs = jnp.where(mask, jnp.exp(masked - top[..., None]), 0.0)
        den = lax.optimization_barrier(jnp.sum(probs, axis=-1))
        acc = jnp.einsum('kgts,skd->kgtd', probs.astype(jnp.bfloat16).astype(jnp.float32), values_f, precision=HIGH)
        out = acc / den[..., None]
        return out.transpose(2, 0, 1, 3).reshape(TOK_DEV, H * HD).astype(jnp.bfloat16)
    attended = lax.map(shard, jnp.arange(N_CTX, dtype=jnp.int32)).reshape(SEQ, H * HD)
    return (mixed, attended)
```

```python
import functools
import math

import jax
import jax.numpy as jnp
from jax import lax
from jax.experimental import pallas as pl
from jax.experimental.pallas import tpu as pltpu
from jax.sharding import Mesh
from jax.sharding import PartitionSpec as P

HD = 128
TOK = 128
HEADS = 16
HALF = 8
WIDTH = HEADS * HD
GROUP = 8
EPS = 1e-06
SCALE2 = math.log2(math.e) / math.sqrt(HD)
NEG = -1e30
MESH = pl.DeviceIdType.MESH
BF = jnp.bfloat16
F32 = jnp.float32
NY, NZ = 4, 8
UNITS = NY * NZ
STEP_UNITS = 4
SHARDS = 2 * STEP_UNITS
KEYS = SHARDS * TOK
STEPS = UNITS // STEP_UNITS
CHUNKS = 2 * STEPS


def ring_next(r, size, tie_up):
    r = r % size
    half = size // 2

    def wanted(distance, up):
        return distance < half or (distance == half and up == tie_up)

    if r == 0:
        return [s for s, up in ((-1, True), (1, False)) if wanted(1, up)]
    if r < half or (r == half and tie_up):
        return [-1] if wanted(r + 1, True) else []
    return [1] if wanted(size - r + 1, False) else []


def sends_of(block):
    dy, dz = block
    out = []
    if dy == 0:
        out += [("z", s) for s in ring_next(dz, NZ, True)]
    out += [("y", s) for s in ring_next(dy, NY, dz % 2 == 0)]
    return out


def plan():
    wire, hop, tick, first = 2.8, 1.8, 2.3, 0.0
    arrival = {(0, 0): 0.0}
    free = {("z", -1): 0.0, ("z", 1): 0.0, ("y", -1): 0.0, ("y", 1): 0.0}
    waiting = {key: [] for key in free}
    held, order, chunks = set(), [], []
    k = 0
    while len(held) < UNITS or any(waiting.values()):
        now = first + k * tick
        waits, starts = [], []
        ready = sorted((b for b in arrival if b not in held and arrival[b] <= now), key=lambda b: arrival[b])
        for b in ready:
            held.add(b)
            order.append(b)
            waits.append(b)
            for way in sends_of(b):
                waiting[way].append(b)
        for way, queue in waiting.items():
            while queue and free[way] < now + tick:
                b = queue.pop(0)
                axis, s = way
                dy, dz = b
                target = ((dy - s) % NY, dz) if axis == "y" else (dy, (dz - s) % NZ)
                free[way] = max(free[way], now) + wire
                arrival[target] = free[way] + hop
                starts.append((b, way, target))
        chunks.append((waits, starts))
        k += 1
    return order, chunks


ORDER, PLAN = plan()
UNIT_AT = {block: place for place, block in enumerate(ORDER)}


def schedule():
    held_at = {b: k for k, (waits, _) in enumerate(PLAN) for b in waits}
    ahead = [([], []) for _ in range(CHUNKS + 1)]
    k = 0
    for c in range(CHUNKS):
        step = c // 2
        need = max(held_at[b] for b in ORDER[step * STEP_UNITS : (step + 1) * STEP_UNITS])
        last = max(need, c)
        while k <= last and k < len(PLAN):
            ahead[c][0].append(k)
            k += 1
    while k < len(PLAN):
        ahead[CHUNKS][0].append(k)
        k += 1
    return [a[0] for a in ahead]


AHEAD = schedule()


def kernel(
    q_hbm, k_hbm, v_hbm, gate_hbm, queries_hbm, keys_hbm, values_hbm, decay_ref, gain_ref, order_ref,
    mixed_ref, attended_ref,
    qx, kx, vx, gx, qs, buf, qaug, kaug, vaug, top, acc, cum, state, dec, lin,
    s_out, s_in, z_out, z_in, edge, y_out, y_in, p_out, p_in, c_out, carr_a, carr_b, x_out, x_in,
    shard_of, load_sem, kv_load_sem, recv_sem, send_sem, part_sem, small_send, small_recv,
):
    me_y, me_z, me_c, me_x = (lax.axis_index(n) for n in ("y", "z", "c", "x"))
    other = 1 - me_c
    first = me_c == 0

    def at(y=None, z=None, c=None, x=None):
        return (
            me_y if y is None else lax.rem(me_y + y + NY, NY),
            me_z if z is None else lax.rem(me_z + z + NZ, NZ),
            me_c if c is None else other,
            me_x if x is None else lax.rem(me_x + x + 4, 4),
        )

    peers = [at(z=d) for d in range(1, NZ)] + [at(y=d) for d in range(1, NY)]
    peers += [at(x=d) for d in range(1, 4)] + [at(c=1)]

    loads = [
        pltpu.make_async_copy(src, dst, load_sem.at[n])
        for n, (src, dst) in enumerate(
            ((k_hbm, kx), (v_hbm, vx), (q_hbm, qx), (queries_hbm, qs), (gate_hbm, gx))
        )
    ]
    kv_loads = []
    for n, src in enumerate((keys_hbm, values_hbm)):
        for g in range(2):
            kv_loads.append(
                pltpu.make_async_copy(
                    src.at[:, g * HD : (g + 1) * HD], buf.at[0, 2 * n + g], kv_load_sem.at[2 * n + g]
                )
            )
    barrier = pltpu.get_barrier_semaphore()
    for peer in peers:
        pl.semaphore_signal(barrier, inc=1, device_id=peer, device_id_type=MESH)
    for load in kv_loads + loads:
        load.start()

    def remote(src, dst, send, recv, device):
        return pltpu.make_async_remote_copy(
            src_ref=src, dst_ref=dst, send_sem=send, recv_sem=recv, device_id=device, device_id_type=MESH
        )

    send_place = {}
    for _, starts in PLAN:
        for b, way, target in starts:
            send_place[(b, way)] = len(send_place)

    def block_copy(b, way, target):
        axis, s = way
        device = at(y=s) if axis == "y" else at(z=s)
        return remote(
            buf.at[2 * UNIT_AT[b]], buf.at[2 * UNIT_AT[target]],
            send_sem.at[send_place[(b, way)]], recv_sem.at[2 * UNIT_AT[target]], device,
        )

    def partner_copy(b):
        u = UNIT_AT[b]
        return remote(buf.at[2 * u], buf.at[2 * u + 1], part_sem.at[u], recv_sem.at[2 * u + 1], at(c=1))

    def arrived(place):
        return remote(buf.at[place], buf.at[place], part_sem.at[0], recv_sem.at[place], at(c=1))

    def communicate(k):
        waits, starts = PLAN[k]
        for b in waits:
            if b != (0, 0):
                arrived(2 * UNIT_AT[b]).wait_recv()
            partner_copy(b).start()
        for b, way, target in starts:
            block_copy(b, way, target).start()

    x = decay_ref[...]
    lane = lax.broadcasted_iota(jnp.int32, (HEADS, TOK), 1)
    for s in (1, 2, 4, 8, 16, 32, 64):
        x = x + jnp.where(lane >= s, pltpu.roll(x, s, axis=1), 0.0)
    cum[...] = x

    row_i = lax.broadcasted_iota(jnp.int32, (TOK, TOK), 0)
    col_i = lax.broadcasted_iota(jnp.int32, (TOK, TOK), 1)
    lower = row_i >= col_i
    head_rows = lax.broadcasted_iota(jnp.int32, (16, HD), 0)

    def columns(h):
        return pl.ds(pl.multiple_of(h * HD, HD), HD)

    def cum_of(h):
        rows = jnp.broadcast_to(cum[pl.ds(h, 1), :], (TOK, TOK))
        return rows, jnp.transpose(rows)

    def silu(v):
        v = v.astype(F32)
        return (v / (1.0 + jnp.exp(-v))).astype(BF)

    def pack_decay(d):
        hi = d.astype(BF)
        rest = d - hi.astype(F32)
        mid = rest.astype(BF)
        low = (rest - mid.astype(F32)).astype(BF)
        return jnp.where(
            head_rows == 0, hi.astype(F32), jnp.where(head_rows == 1, mid.astype(F32), low.astype(F32))
        ).astype(BF)

    def unpack_decay(rows):
        r = rows.astype(F32)
        return r[0:1] + r[1:2] + r[2:3]

    loads[0].wait()
    loads[1].wait()

    def local_state(h, carry):
        cols = columns(h)
        _, cb = cum_of(h)
        kb = silu(kx[:, cols])
        vb = silu(vx[:, cols])
        kx[:, cols] = kb
        vx[:, cols] = vb
        last = cb[TOK - 1 : TOK, :]
        kdec = (kb.astype(F32) * jnp.exp(last - cb)).astype(BF)
        s = lax.dot_general(kdec, vb, (((0,), (0,)), ((), ())), preferred_element_type=F32)
        state[h] = s
        d = jnp.exp(last)
        dec[h] = jnp.broadcast_to(d, (8, HD))
        return carry

    lax.fori_loop(0, HEADS, local_state, 0)

    def to_partner(r, carry):
        h = other * HALF + r
        s_out[r, 0:HD] = state[h].astype(BF)
        s_out[r, HD : HD + 16] = pack_decay(dec[h][0:1])
        return carry

    lax.fori_loop(0, HALF, to_partner, 0)
    pl.semaphore_wait(barrier, len(peers))
    state_copy = remote(s_out, s_in, small_send.at[0], small_recv.at[0], at(c=1))
    state_copy.start()
    for load in kv_loads:
        load.wait()
    communicate(0)

    loads[3].wait()
    unit = jnp.where(row_i == col_i, 1.0, 0.0).astype(BF)

    def spread(h, carry):
        rows = pl.ds(pl.multiple_of(h * TOK, TOK), TOK)
        qaug[rows, 0:HD] = qs[:, columns(h)]
        qaug[rows, HD : 2 * HD] = unit
        top[rows, :] = jnp.full((TOK, HD), NEG, F32)
        acc[rows, :] = jnp.zeros((TOK, 2 * HD), F32)
        return carry

    lax.fori_loop(0, HEADS, spread, 0)
    for u, (dy, dz) in enumerate(ORDER):
        chip = lax.rem(me_y + dy, NY) * NZ + lax.rem(me_z + dz, NZ)
        shard_of[2 * u] = 2 * chip + me_c
        shard_of[2 * u + 1] = 2 * chip + other
    my_shard = order_ref[0]
    above = jnp.where(row_i > col_i, NEG, 0.0)

    def softmax(i):
        g = lax.rem(i, 2)
        base = lax.div(i, 2) * SHARDS
        for s in range(SHARDS):
            rows = slice(s * TOK, (s + 1) * TOK)
            shard = shard_of[base + s]
            kaug[rows, 0:HD] = buf[base + s, g]
            vaug[rows, :] = buf[base + s, 2 + g]
            whole = jnp.where(shard > my_shard, NEG, 0.0)
            part = jnp.where(shard == my_shard, 1.0, 0.0)
            kaug[rows, HD : 2 * HD] = (above * part + whole).astype(BF)
        rows = pl.ds(pl.multiple_of(g * GROUP * TOK, GROUP * TOK), GROUP * TOK)
        sc = lax.dot_general(
            qaug[rows, :], kaug[...], (((1,), (1,)), ((), ())), preferred_element_type=F32
        )
        old = top[rows, :]
        new = jnp.maximum(old, jnp.max(sc, axis=1, keepdims=True))
        w = jnp.exp2(sc * SCALE2 - jnp.tile(new * SCALE2, (1, SHARDS)))
        alpha = jnp.exp2((old - new) * SCALE2)
        pv = jnp.dot(w.astype(BF), vaug[...], preferred_element_type=F32)
        acc[rows, 0:HD] = acc[rows, 0:HD] * alpha + pv
        den = w[:, 0:HD]
        for s in range(1, SHARDS):
            den = den + w[:, s * HD : (s + 1) * HD]
        acc[rows, HD : 2 * HD] = acc[rows, HD : 2 * HD] * alpha + den
        top[rows, :] = new

    def intra():
        loads[2].wait()

        def one(h, carry):
            cols = columns(h)
            rb, cb = cum_of(h)
            qb = silu(qx[:, cols])
            sc = lax.dot_general(qb, kx[:, cols], (((1,), (1,)), ((), ())), preferred_element_type=F32)
            decay = jnp.where(lower, jnp.exp(jnp.where(lower, cb - rb, 0.0)), 0.0)
            w = (sc * decay).astype(BF)
            lin[:, cols] = jnp.dot(w, vx[:, cols], preferred_element_type=F32)
            qx[:, cols] = (qb.astype(F32) * jnp.exp(cb)).astype(BF)
            return carry

        lax.fori_loop(0, HEADS, one, 0)

    def z_copy(d):
        head = lax.rem(me_z + d, NZ)
        return remote(z_out.at[head], z_in.at[NZ - d], small_send.at[d], small_recv.at[NZ - d], at(z=d))

    def z_arrival(d):
        return remote(z_out.at[0], z_in.at[d], small_send.at[0], small_recv.at[d], at(z=d))

    def chip_totals():
        remote(s_out, s_in, small_send.at[0], small_recv.at[0], at(c=1)).wait_recv()

        def one(r, carry):
            h = me_c * HALF + r
            mine, d_mine = state[h], dec[h][0:1]
            theirs = s_in[r, 0:HD].astype(F32)
            d_theirs = unpack_decay(s_in[r, HD : HD + 16])
            total = jnp.where(first, d_theirs, 1.0) * mine + jnp.where(first, 1.0, d_mine) * theirs
            z_out[r, 0:HD] = total.astype(BF)
            z_out[r, HD : HD + 16] = pack_decay(d_mine * d_theirs)
            return carry

        lax.fori_loop(0, HALF, one, 0)
        for d in range(1, NZ):
            z_copy(d).start()

    def y_copy(d):
        return remote(y_out, y_in.at[NY - d], small_send.at[8 + d], small_recv.at[8 + NY - d], at(y=d))

    def y_arrival(d):
        return remote(y_out, y_in.at[d], small_send.at[0], small_recv.at[8 + d], at(y=d))

    def row_scan():
        for d in range(1, NZ):
            z_arrival(d).wait_recv()
        z_in[0] = z_out[me_z]

        def one(k, carry):
            e, a = carry
            rel = lax.rem(k - me_z + NZ, NZ)
            edge[k, 0:HD] = e
            edge[k, HD : HD + 8] = jnp.broadcast_to(a, (8, HD))
            d = unpack_decay(z_in[rel, HD : HD + 16])
            return d * e + z_in[rel, 0:HD].astype(F32), a * d

        e, a = lax.fori_loop(0, NZ, one, (jnp.zeros((HD, HD), F32), jnp.ones((1, HD), F32)))
        y_out[0:HD] = e
        y_out[HD : HD + 8] = jnp.broadcast_to(a, (8, HD))
        y_in[0] = jnp.zeros((HD + 8, HD), F32)
        for d in range(1, NY):
            y_copy(d).start()

    def p_copy(d):
        chip = lax.rem(me_z + d, NZ)
        return remote(p_out.at[chip], p_in.at[NZ - d], small_send.at[16 + d], small_recv.at[16 + NZ - d], at(z=d))

    def p_arrival(d):
        return remote(p_out.at[0], p_in.at[d], small_send.at[0], small_recv.at[16 + d], at(z=d))

    def prefixes():
        for d in range(1, NY):
            y_arrival(d).wait_recv()
        carry = jnp.zeros((HD, HD), F32)
        for k in range(NY - 1):
            rel = lax.rem(k - me_y + NY, NY)
            grown = y_in[rel, HD : HD + 1] * carry + y_in[rel, 0:HD]
            carry = jnp.where(k < me_y, grown, carry)

        for k in range(NZ):
            p_out[k] = (edge[k, 0:HD] + edge[k, HD : HD + 1] * carry).astype(BF)
        for d in range(1, NZ):
            p_copy(d).start()

    def carries():
        for d in range(1, NZ):
            p_arrival(d).wait_recv()
        p_in[0] = p_out[me_z]

        def one(r, carry):
            h = me_c * HALF + r
            before = p_in[lax.rem(r - me_z + NZ, NZ)].astype(F32)
            d_theirs = unpack_decay(s_in[r, HD : HD + 16])
            d = jnp.where(first, dec[h][0:1], d_theirs)
            s = jnp.where(first, state[h], s_in[r, 0:HD].astype(F32))
            after = d * before + s
            carr_a[r] = jnp.where(first, before, after).astype(BF)
            c_out[r] = jnp.where(first, after, before).astype(BF)
            return carry

        lax.fori_loop(0, HALF, one, 0)
        remote(c_out, carr_b, small_send.at[24], small_recv.at[24], at(c=1)).start()

    def x_copy(d):
        return remote(x_out, x_in.at[4 - d], small_send.at[24 + d], small_recv.at[24 + 4 - d], at(x=d))

    def x_arrival(d):
        return remote(x_out, x_in.at[d], small_send.at[0], small_recv.at[24 + d], at(x=d))

    def inter():
        def half(source, start):
            def one(r, total):
                cols = columns(start + r)
                value = lin[:, cols] + jnp.dot(qx[:, cols], source[r], preferred_element_type=F32)
                lin[:, cols] = value
                return total + value * value

            return one

        total = lax.fori_loop(0, HALF, half(carr_a, me_c * HALF), jnp.zeros((TOK, HD), F32))
        remote(c_out, carr_b, small_send.at[24], small_recv.at[24], at(c=1)).wait_recv()
        total = lax.fori_loop(0, HALF, half(carr_b, other * HALF), total)
        x_out[...] = total
        for d in range(1, 4):
            x_copy(d).start()

    def finish():
        loads[4].wait()
        total = x_out[...]
        for d in range(1, 4):
            x_arrival(d).wait_recv()
            total = total + x_in[d]
        inv = lax.rsqrt(jnp.sum(total, axis=1, keepdims=True) / (4 * WIDTH) + EPS)
        inv = jnp.broadcast_to(inv, (TOK, HD))

        def one(h, carry):
            cols = columns(h)
            g = gx[:, cols].astype(F32)
            gated = 1.0 / (1.0 + jnp.exp(-g))
            mixed_ref[:, cols] = (lin[:, cols] * inv * gain_ref[:, cols] * gated).astype(BF)
            return carry

        lax.fori_loop(0, HEADS, one, 0)

    TASKS = {0: intra, 1: chip_totals, 4: row_scan, 7: prefixes, 10: carries, 12: inter, 14: finish}

    def chunk(i, carry):
        for c in range(CHUNKS):

            @pl.when(i == c)
            def _(c=c):
                for k in AHEAD[c]:
                    if k > 0:
                        communicate(k)
                if c % 2 == 0:
                    for u in range(c // 2 * STEP_UNITS, (c // 2 + 1) * STEP_UNITS):
                        arrived(2 * u + 1).wait_recv()
                if c in TASKS:
                    TASKS[c]()

        softmax(i)
        return carry

    lax.fori_loop(0, CHUNKS, chunk, 0)
    for k in AHEAD[CHUNKS]:
        communicate(k)

    def result(h, carry):
        rows = pl.ds(pl.multiple_of(h * TOK, TOK), TOK)
        den = jnp.sum(acc[rows, HD : 2 * HD], axis=1, keepdims=True)
        attended_ref[:, columns(h)] = (acc[rows, 0:HD] / den).astype(BF)
        return carry

    lax.fori_loop(0, HEADS, result, 0)

    state_copy.wait_send()
    for d in range(1, NZ):
        z_copy(d).wait_send()
        p_copy(d).wait_send()
    for d in range(1, NY):
        y_copy(d).wait_send()
    remote(c_out, carr_b, small_send.at[24], small_recv.at[24], at(c=1)).wait_send()
    for d in range(1, 4):
        x_copy(d).wait_send()
    for waits, starts in PLAN:
        for b in waits:
            partner_copy(b).wait_send()
        for b, way, target in starts:
            block_copy(b, way, target).wait_send()


def body(q_lin, k_lin, v_lin, log_decay, gate, norm_gain, queries, keys, values, order):
    vmem = pl.BlockSpec(memory_space=pltpu.VMEM)
    hbm = pl.BlockSpec(memory_space=pl.ANY)
    out = jax.ShapeDtypeStruct((TOK, WIDTH), BF)
    n_sends = sum(len(starts) for _, starts in PLAN)
    wide = pltpu.VMEM((TOK, WIDTH), BF)
    return pl.pallas_call(
        kernel,
        out_shape=(out, out),
        in_specs=[hbm] * 7 + [vmem, vmem, pl.BlockSpec(memory_space=pltpu.SMEM)],
        out_specs=(vmem, vmem),
        scratch_shapes=[
            wide, wide, wide, wide, wide,
            pltpu.VMEM((2 * UNITS, 4, TOK, HD), BF),
            pltpu.VMEM((HEADS * TOK, 2 * HD), BF),
            pltpu.VMEM((KEYS, 2 * HD), BF),
            pltpu.VMEM((KEYS, HD), BF),
            pltpu.VMEM((HEADS * TOK, HD), F32),
            pltpu.VMEM((HEADS * TOK, 2 * HD), F32),
            pltpu.VMEM((HEADS, TOK), F32),
            pltpu.VMEM((HEADS, HD, HD), F32),
            pltpu.VMEM((HEADS, 8, HD), F32),
            pltpu.VMEM((TOK, WIDTH), F32),
            pltpu.VMEM((HALF, HD + 16, HD), BF),
            pltpu.VMEM((HALF, HD + 16, HD), BF),
            pltpu.VMEM((NZ, HD + 16, HD), BF),
            pltpu.VMEM((NZ, HD + 16, HD), BF),
            pltpu.VMEM((NZ, HD + 8, HD), F32),
            pltpu.VMEM((HD + 8, HD), F32),
            pltpu.VMEM((NY, HD + 8, HD), F32),
            pltpu.VMEM((NZ, HD, HD), BF),
            pltpu.VMEM((NZ, HD, HD), BF),
            pltpu.VMEM((HALF, HD, HD), BF),
            pltpu.VMEM((HALF, HD, HD), BF),
            pltpu.VMEM((HALF, HD, HD), BF),
            pltpu.VMEM((TOK, HD), F32),
            pltpu.VMEM((4, TOK, HD), F32),
            pltpu.SMEM((2 * UNITS,), jnp.int32),
            pltpu.SemaphoreType.DMA((5,)),
            pltpu.SemaphoreType.DMA((4,)),
            pltpu.SemaphoreType.DMA((2 * UNITS,)),
            pltpu.SemaphoreType.DMA((n_sends,)),
            pltpu.SemaphoreType.DMA((UNITS,)),
            pltpu.SemaphoreType.DMA((28,)),
            pltpu.SemaphoreType.DMA((28,)),
        ],
        compiler_params=pltpu.CompilerParams(
            collective_id=0, has_side_effects=True, vmem_limit_bytes=62 * 2**20
        ),
    )(
        q_lin, k_lin, v_lin, gate, queries, keys, values, log_decay, norm_gain.reshape(1, WIDTH), order
    )


def solution(mesh):
    finer = Mesh(
        mesh.devices.reshape(NY, NZ, 2, mesh.shape["head"]), ("y", "z", "c", "x")
    )
    rows = ("y", "z", "c")
    tile = P(rows, "x")
    return jax.shard_map(
        body,
        mesh=finer,
        in_specs=(tile, tile, tile, P("x", rows), tile, P("x"), tile, tile, tile, P(rows)),
        out_specs=(tile, tile),
        check_vma=False,
    )
```

```python
import functools
import math

import jax
import jax.numpy as jnp
from jax import lax
from jax.experimental import pallas as pl
from jax.experimental.pallas import tpu as pltpu
from jax.sharding import Mesh
from jax.sharding import PartitionSpec as P

HD = 128
TOK = 128
HEADS = 16
HALF = 8
WIDTH = HEADS * HD
GROUP = 8
EPS = 1e-06
SCALE2 = math.log2(math.e) / math.sqrt(HD)
NEG = -1e30
MESH = pl.DeviceIdType.MESH
BF = jnp.bfloat16
F32 = jnp.float32
NY, NZ = 4, 8
UNITS = NY * NZ
STEP_UNITS = 4
SHARDS = 2 * STEP_UNITS
KEYS = SHARDS * TOK
STEPS = UNITS // STEP_UNITS
CHUNKS = 2 * STEPS


def ring_next(r, size, tie_up):
    r = r % size
    half = size // 2

    def wanted(distance, up):
        return distance < half or (distance == half and up == tie_up)

    if r == 0:
        return [s for s, up in ((-1, True), (1, False)) if wanted(1, up)]
    if r < half or (r == half and tie_up):
        return [-1] if wanted(r + 1, True) else []
    return [1] if wanted(size - r + 1, False) else []


PART_SIZES = (4,)
RATE, LATENCY = 104.0, 1.8
CORE_RATE, CORE_LATENCY = 400.0, 1.1
SOFTMAX, ISSUE, AHEAD_TIME = 1.9, 0.04, 2.0
COST = {"intra": 2.0, "chip_totals": 0.7, "row_scan": 0.7, "prefixes": 0.4, "carries": 0.7, "inter": 1.2, "finish": 0.6}
MESSAGES = {
    "chip_totals": [(("z", 1), 36 * 8), (("z", -1), 36 * 8)],
    "row_scan": [(("y", 1), 70 * 2), (("y", -1), 70 * 2)],
    "prefixes": [(("z", 1), 32 * 8), (("z", -1), 32 * 8)],
    "carries": [(("c", 0), 256)],
    "inter": [(("x", 1), 64 * 2)],
    "finish": [],
}


def sends_of(item):
    part, dy, dz = item
    out = []
    if part == 0:
        if dy == 0:
            out += [("z", s) for s in ring_next(dz, NZ, True)]
        out += [("y", s) for s in ring_next(dy, NY, dz % 2 == 0)]
    else:
        if dz == 0:
            out += [("y", s) for s in ring_next(dy, NY, True)]
        out += [("z", s) for s in ring_next(dz, NZ, dy % 2 == 0)]
    return out


def plan():
    parts = range(len(PART_SIZES))
    free = {}
    arrival = {}
    queues = {(axis, s): [] for axis in "zy" for s in (-1, 1)}
    held, order, chunks, ops = set(), [], [], []
    pending = ["intra"] + list(MESSAGES)
    due = {"intra": 0.0}
    now = 0.0

    def use(way, size):
        rate, latency = (CORE_RATE, CORE_LATENCY) if way[0] == "c" else (RATE / 2, LATENCY)
        free[way] = max(free.get(way, 0.0), now) + size * 1.024 / rate
        return free[way] + latency

    def issue():
        for way, queue in queues.items():
            while queue and free.get(way, 0.0) < now + AHEAD_TIME:
                item = queue.pop(0)
                axis, s = way
                part, dy, dz = item
                target = (part, (dy - s) % NY, dz) if axis == "y" else (part, dy, (dz - s) % NZ)
                arrival[target] = use(way, 32 * PART_SIZES[part])
                ops.append(("start", item, way, target))

    def take(item):
        held.add(item)
        for way in sends_of(item):
            queues[way].append(item)
        issue()
        arrival[item + (1,)] = use(("c", 0), 32 * PART_SIZES[item[0]])
        ops.append(("partner", item))
        if all((p,) + item[1:] in held for p in parts):
            order.append(item[1:])

    due["chip_totals"] = use(("c", 0), 288)
    for p in parts:
        ops.append(("take", (p, 0, 0)))
        take((p, 0, 0))
    done = 0
    while done < CHUNKS or pending:
        while True:
            if pending and due.get(pending[0], 1e9) <= now:
                name = pending.pop(0)
                ops.append(("task", name))
                now += COST[name]
                if pending:
                    sent = [use(way, size) for way, size in MESSAGES.get(name, [])]
                    if sent:
                        due[pending[0]] = max(sent)
                continue
            came = sorted((i for i in arrival if len(i) == 3 and i not in held and arrival[i] <= now), key=lambda i: arrival[i])
            if came:
                now += ISSUE
                ops.append(("take", came[0]))
                take(came[0])
                continue
            break
        issue()
        group = order[done // 2 * STEP_UNITS : (done // 2 + 1) * STEP_UNITS]
        needs = [(p,) + b + (1,) for b in group for p in parts]
        if done < CHUNKS and len(group) == STEP_UNITS and all(arrival[i] <= now for i in needs):
            chunks.append(ops)
            ops = []
            now += SOFTMAX
            done += 1
            continue
        if done == CHUNKS and not pending:
            break
        later = [arrival[i] for i in arrival if arrival[i] > now]
        if pending and due.get(pending[0], 1e9) > now:
            later.append(due[pending[0]])
        later += [free[w] - AHEAD_TIME + 0.001 for w, q in queues.items() if q and free[w] - AHEAD_TIME > now - 0.001]
        if not later:
            break
        now = max(min(later), now + 1e-6)
    chunks.append(ops)
    return order, chunks


ORDER, PLAN = plan()
UNIT_AT = {block: place for place, block in enumerate(ORDER)}
BOUNDS = [sum(PART_SIZES[:p]) for p in range(len(PART_SIZES) + 1)]


def kernel(
    q_hbm, k_hbm, v_hbm, gate_hbm, queries_hbm, keys_hbm, values_hbm, decay_ref, gain_ref, order_ref,
    mixed_ref, attended_ref,
    qx, kx, vx, gx, qs, buf, qaug, kaug, vaug, top, acc, cum, state, dec, lin,
    s_out, s_in, z_out, z_in, edge, y_out, y_in, p_out, p_in, c_out, carr_a, carr_b, x_out, x_in,
    shard_of, load_sem, kv_load_sem, recv_sem, send_sem, part_sem, small_send, small_recv,
):
    me_y, me_z, me_c, me_x = (lax.axis_index(n) for n in ("y", "z", "c", "x"))
    other = 1 - me_c
    first = me_c == 0

    def at(y=None, z=None, c=None, x=None):
        return (
            me_y if y is None else lax.rem(me_y + y + NY, NY),
            me_z if z is None else lax.rem(me_z + z + NZ, NZ),
            me_c if c is None else other,
            me_x if x is None else lax.rem(me_x + x + 4, 4),
        )

    peers = [at(z=d) for d in range(1, NZ)] + [at(y=d) for d in range(1, NY)]
    peers += [at(x=d) for d in range(1, 4)] + [at(c=1)]

    loads = [
        pltpu.make_async_copy(src, dst, load_sem.at[n])
        for n, (src, dst) in enumerate(
            ((k_hbm, kx), (v_hbm, vx), (q_hbm, qx), (queries_hbm, qs), (gate_hbm, gx))
        )
    ]
    kv_loads = []
    for n, src in enumerate((keys_hbm, values_hbm)):
        for g in range(2):
            kv_loads.append(
                pltpu.make_async_copy(
                    src.at[:, g * HD : (g + 1) * HD], buf.at[0, 2 * n + g], kv_load_sem.at[2 * n + g]
                )
            )
    barrier = pltpu.get_barrier_semaphore()
    for peer in peers:
        pl.semaphore_signal(barrier, inc=1, device_id=peer, device_id_type=MESH)
    for load in kv_loads + loads:
        load.start()

    def remote(src, dst, send, recv, device):
        return pltpu.make_async_remote_copy(
            src_ref=src, dst_ref=dst, send_sem=send, recv_sem=recv, device_id=device, device_id_type=MESH
        )

    send_place = {}
    for ops in PLAN:
        for op in ops:
            if op[0] == "start":
                send_place[op[1:3]] = len(send_place)

    def slot(item, partner):
        return 2 * UNIT_AT[item[1:]] + partner

    def part_of(item, partner):
        return buf.at[slot(item, partner), BOUNDS[item[0]] : BOUNDS[item[0] + 1]]

    def landed(item, partner):
        return recv_sem.at[item[0] * 2 * UNITS + slot(item, partner)]

    def block_copy(item, way, target):
        axis, s = way
        device = at(y=s) if axis == "y" else at(z=s)
        return remote(
            part_of(item, 0), part_of(target, 0), send_sem.at[send_place[(item, way)]], landed(target, 0), device
        )

    def partner_copy(item):
        sem = part_sem.at[item[0] * UNITS + UNIT_AT[item[1:]]]
        return remote(part_of(item, 0), part_of(item, 1), sem, landed(item, 1), at(c=1))

    def arrived(item, partner):
        return remote(part_of(item, partner), part_of(item, partner), part_sem.at[0], landed(item, partner), at(c=1))

    def perform(ops):
        for op in ops:
            if op[0] == "take":
                if op[1][1:] != (0, 0):
                    arrived(op[1], 0).wait_recv()
            elif op[0] == "start":
                block_copy(*op[1:]).start()
            elif op[0] == "partner":
                partner_copy(op[1]).start()
            else:
                tasks[op[1]]()

    x = decay_ref[...]
    lane = lax.broadcasted_iota(jnp.int32, (HEADS, TOK), 1)
    for s in (1, 2, 4, 8, 16, 32, 64):
        x = x + jnp.where(lane >= s, pltpu.roll(x, s, axis=1), 0.0)
    cum[...] = x

    row_i = lax.broadcasted_iota(jnp.int32, (TOK, TOK), 0)
    col_i = lax.broadcasted_iota(jnp.int32, (TOK, TOK), 1)
    lower = row_i >= col_i
    head_rows = lax.broadcasted_iota(jnp.int32, (16, HD), 0)

    def columns(h):
        return pl.ds(pl.multiple_of(h * HD, HD), HD)

    def cum_of(h):
        rows = jnp.broadcast_to(cum[pl.ds(h, 1), :], (TOK, TOK))
        return rows, jnp.transpose(rows)

    def silu(v):
        v = v.astype(F32)
        return (v / (1.0 + jnp.exp(-v))).astype(BF)

    def pack_decay(d):
        hi = d.astype(BF)
        rest = d - hi.astype(F32)
        mid = rest.astype(BF)
        low = (rest - mid.astype(F32)).astype(BF)
        return jnp.where(
            head_rows == 0, hi.astype(F32), jnp.where(head_rows == 1, mid.astype(F32), low.astype(F32))
        ).astype(BF)

    def unpack_decay(rows):
        r = rows.astype(F32)
        return r[0:1] + r[1:2] + r[2:3]

    loads[0].wait()
    loads[1].wait()

    def local_state(h, carry):
        cols = columns(h)
        _, cb = cum_of(h)
        kb = silu(kx[:, cols])
        vb = silu(vx[:, cols])
        kx[:, cols] = kb
        vx[:, cols] = vb
        last = cb[TOK - 1 : TOK, :]
        kdec = (kb.astype(F32) * jnp.exp(last - cb)).astype(BF)
        s = lax.dot_general(kdec, vb, (((0,), (0,)), ((), ())), preferred_element_type=F32)
        state[h] = s
        d = jnp.exp(last)
        dec[h] = jnp.broadcast_to(d, (8, HD))
        return carry

    lax.fori_loop(0, HEADS, local_state, 0, unroll=True)

    def to_partner(r, carry):
        h = other * HALF + r
        s_out[r, 0:HD] = state[h].astype(BF)
        s_out[r, HD : HD + 16] = pack_decay(dec[h][0:1])
        return carry

    lax.fori_loop(0, HALF, to_partner, 0, unroll=True)
    pl.semaphore_wait(barrier, len(peers))
    state_copy = remote(s_out, s_in, small_send.at[0], small_recv.at[0], at(c=1))
    state_copy.start()
    for load in kv_loads:
        load.wait()
    opening = next(n for n, op in enumerate(PLAN[0]) if op[0] == "task")
    perform(PLAN[0][:opening])

    loads[3].wait()
    unit = jnp.where(row_i == col_i, 1.0, 0.0).astype(BF)

    def spread(h, carry):
        rows = pl.ds(pl.multiple_of(h * TOK, TOK), TOK)
        qaug[rows, 0:HD] = qs[:, columns(h)]
        qaug[rows, HD : 2 * HD] = unit
        top[rows, :] = jnp.full((TOK, HD), NEG, F32)
        acc[rows, :] = jnp.zeros((TOK, 2 * HD), F32)
        return carry

    lax.fori_loop(0, HEADS, spread, 0)
    for u, (dy, dz) in enumerate(ORDER):
        chip = lax.rem(me_y + dy, NY) * NZ + lax.rem(me_z + dz, NZ)
        shard_of[2 * u] = 2 * chip + me_c
        shard_of[2 * u + 1] = 2 * chip + other
    my_shard = order_ref[0]
    above = jnp.where(row_i > col_i, NEG, 0.0)

    def softmax(i):
        g = lax.rem(i, 2)
        base = lax.div(i, 2) * SHARDS
        for s in range(SHARDS):
            rows = slice(s * TOK, (s + 1) * TOK)
            shard = shard_of[base + s]
            kaug[rows, 0:HD] = buf[base + s, g]
            vaug[rows, :] = buf[base + s, 2 + g]
            whole = jnp.where(shard > my_shard, NEG, 0.0)
            part = jnp.where(shard == my_shard, 1.0, 0.0)
            kaug[rows, HD : 2 * HD] = (above * part + whole).astype(BF)
        rows = pl.ds(pl.multiple_of(g * GROUP * TOK, GROUP * TOK), GROUP * TOK)
        sc = lax.dot_general(
            qaug[rows, :], kaug[...], (((1,), (1,)), ((), ())), preferred_element_type=F32
        )
        old = top[rows, :]
        new = jnp.maximum(old, jnp.max(sc, axis=1, keepdims=True))
        w = jnp.exp2(sc * SCALE2 - jnp.tile(new * SCALE2, (1, SHARDS)))
        alpha = jnp.exp2((old - new) * SCALE2)
        pv = jnp.dot(w.astype(BF), vaug[...], preferred_element_type=F32)
        acc[rows, 0:HD] = acc[rows, 0:HD] * alpha + pv
        den = w[:, 0:HD]
        for s in range(1, SHARDS):
            den = den + w[:, s * HD : (s + 1) * HD]
        acc[rows, HD : 2 * HD] = acc[rows, HD : 2 * HD] * alpha + den
        top[rows, :] = new

    def intra():
        loads[2].wait()

        def one(h, carry):
            cols = columns(h)
            rb, cb = cum_of(h)
            qb = silu(qx[:, cols])
            sc = lax.dot_general(qb, kx[:, cols], (((1,), (1,)), ((), ())), preferred_element_type=F32)
            decay = jnp.where(lower, jnp.exp(jnp.where(lower, cb - rb, 0.0)), 0.0)
            w = (sc * decay).astype(BF)
            lin[:, cols] = jnp.dot(w, vx[:, cols], preferred_element_type=F32)
            qx[:, cols] = (qb.astype(F32) * jnp.exp(cb)).astype(BF)
            return carry

        lax.fori_loop(0, HEADS, one, 0, unroll=True)

    def z_copy(d):
        head = lax.rem(me_z + d, NZ)
        return remote(z_out.at[head], z_in.at[NZ - d], small_send.at[d], small_recv.at[NZ - d], at(z=d))

    def z_arrival(d):
        return remote(z_out.at[0], z_in.at[d], small_send.at[0], small_recv.at[d], at(z=d))

    def chip_totals():
        remote(s_out, s_in, small_send.at[0], small_recv.at[0], at(c=1)).wait_recv()

        def one(r, carry):
            h = me_c * HALF + r
            mine, d_mine = state[h], dec[h][0:1]
            theirs = s_in[r, 0:HD].astype(F32)
            d_theirs = unpack_decay(s_in[r, HD : HD + 16])
            total = jnp.where(first, d_theirs, 1.0) * mine + jnp.where(first, 1.0, d_mine) * theirs
            z_out[r, 0:HD] = total.astype(BF)
            z_out[r, HD : HD + 16] = pack_decay(d_mine * d_theirs)
            return carry

        lax.fori_loop(0, HALF, one, 0, unroll=True)
        for d in range(1, NZ):
            z_copy(d).start()

    def y_copy(d):
        return remote(y_out, y_in.at[NY - d], small_send.at[8 + d], small_recv.at[8 + NY - d], at(y=d))

    def y_arrival(d):
        return remote(y_out, y_in.at[d], small_send.at[0], small_recv.at[8 + d], at(y=d))

    def row_scan():
        for d in range(1, NZ):
            z_arrival(d).wait_recv()
        z_in[0] = z_out[me_z]

        def one(k, carry):
            e, a = carry
            rel = lax.rem(k - me_z + NZ, NZ)
            edge[k, 0:HD] = e
            edge[k, HD : HD + 8] = jnp.broadcast_to(a, (8, HD))
            d = unpack_decay(z_in[rel, HD : HD + 16])
            return d * e + z_in[rel, 0:HD].astype(F32), a * d

        e, a = lax.fori_loop(0, NZ, one, (jnp.zeros((HD, HD), F32), jnp.ones((1, HD), F32)))
        y_out[0:HD] = e
        y_out[HD : HD + 8] = jnp.broadcast_to(a, (8, HD))
        y_in[0] = jnp.zeros((HD + 8, HD), F32)
        for d in range(1, NY):
            y_copy(d).start()

    def p_copy(d):
        chip = lax.rem(me_z + d, NZ)
        return remote(p_out.at[chip], p_in.at[NZ - d], small_send.at[16 + d], small_recv.at[16 + NZ - d], at(z=d))

    def p_arrival(d):
        return remote(p_out.at[0], p_in.at[d], small_send.at[0], small_recv.at[16 + d], at(z=d))

    def prefixes():
        for d in range(1, NY):
            y_arrival(d).wait_recv()
        carry = jnp.zeros((HD, HD), F32)
        for k in range(NY - 1):
            rel = lax.rem(k - me_y + NY, NY)
            grown = y_in[rel, HD : HD + 1] * carry + y_in[rel, 0:HD]
            carry = jnp.where(k < me_y, grown, carry)

        for k in range(NZ):
            p_out[k] = (edge[k, 0:HD] + edge[k, HD : HD + 1] * carry).astype(BF)
        for d in range(1, NZ):
            p_copy(d).start()

    def carries():
        for d in range(1, NZ):
            p_arrival(d).wait_recv()
        p_in[0] = p_out[me_z]

        def one(r, carry):
            h = me_c * HALF + r
            before = p_in[lax.rem(r - me_z + NZ, NZ)].astype(F32)
            d_theirs = unpack_decay(s_in[r, HD : HD + 16])
            d = jnp.where(first, dec[h][0:1], d_theirs)
            s = jnp.where(first, state[h], s_in[r, 0:HD].astype(F32))
            after = d * before + s
            carr_a[r] = jnp.where(first, before, after).astype(BF)
            c_out[r] = jnp.where(first, after, before).astype(BF)
            return carry

        lax.fori_loop(0, HALF, one, 0, unroll=True)
        remote(c_out, carr_b, small_send.at[24], small_recv.at[24], at(c=1)).start()

    def x_copy(d):
        return remote(x_out, x_in.at[4 - d], small_send.at[24 + d], small_recv.at[24 + 4 - d], at(x=d))

    def x_arrival(d):
        return remote(x_out, x_in.at[d], small_send.at[0], small_recv.at[24 + d], at(x=d))

    def inter():
        def half(source, start):
            def one(r, total):
                cols = columns(start + r)
                value = lin[:, cols] + jnp.dot(qx[:, cols], source[r], preferred_element_type=F32)
                lin[:, cols] = value
                return total + value * value

            return one

        total = lax.fori_loop(
            0, HALF, half(carr_a, me_c * HALF), jnp.zeros((TOK, HD), F32), unroll=True
        )
        remote(c_out, carr_b, small_send.at[24], small_recv.at[24], at(c=1)).wait_recv()
        total = lax.fori_loop(0, HALF, half(carr_b, other * HALF), total, unroll=True)
        x_out[...] = total
        for d in range(1, 4):
            x_copy(d).start()

    def finish():
        loads[4].wait()
        total = x_out[...]
        for d in range(1, 4):
            x_arrival(d).wait_recv()
            total = total + x_in[d]
        inv = lax.rsqrt(jnp.sum(total, axis=1, keepdims=True) / (4 * WIDTH) + EPS)
        inv = jnp.broadcast_to(inv, (TOK, HD))

        def one(h, carry):
            cols = columns(h)
            g = gx[:, cols].astype(F32)
            gated = 1.0 / (1.0 + jnp.exp(-g))
            mixed_ref[:, cols] = (lin[:, cols] * inv * gain_ref[:, cols] * gated).astype(BF)
            return carry

        lax.fori_loop(0, HEADS, one, 0, unroll=True)

    tasks = {
        task.__name__: task for task in (intra, chip_totals, row_scan, prefixes, carries, inter, finish)
    }

    def chunk(i, carry):
        for c in range(CHUNKS):

            @pl.when(i == c)
            def _(c=c):
                perform(PLAN[c][opening:] if c == 0 else PLAN[c])
                if c % 2 == 0:
                    for u in range(c // 2 * STEP_UNITS, (c // 2 + 1) * STEP_UNITS):
                        for part in range(len(PART_SIZES)):
                            arrived((part,) + ORDER[u], 1).wait_recv()

        softmax(i)
        return carry

    lax.fori_loop(0, CHUNKS, chunk, 0)
    perform(PLAN[CHUNKS])

    def result(h, carry):
        rows = pl.ds(pl.multiple_of(h * TOK, TOK), TOK)
        den = jnp.sum(acc[rows, HD : 2 * HD], axis=1, keepdims=True)
        attended_ref[:, columns(h)] = (acc[rows, 0:HD] / den).astype(BF)
        return carry

    lax.fori_loop(0, HEADS, result, 0)

    state_copy.wait_send()
    for d in range(1, NZ):
        z_copy(d).wait_send()
        p_copy(d).wait_send()
    for d in range(1, NY):
        y_copy(d).wait_send()
    remote(c_out, carr_b, small_send.at[24], small_recv.at[24], at(c=1)).wait_send()
    for d in range(1, 4):
        x_copy(d).wait_send()
    for ops in PLAN:
        for op in ops:
            if op[0] == "start":
                block_copy(*op[1:]).wait_send()
            elif op[0] == "partner":
                partner_copy(op[1]).wait_send()


def body(q_lin, k_lin, v_lin, log_decay, gate, norm_gain, queries, keys, values, order):
    vmem = pl.BlockSpec(memory_space=pltpu.VMEM)
    hbm = pl.BlockSpec(memory_space=pl.ANY)
    out = jax.ShapeDtypeStruct((TOK, WIDTH), BF)
    n_sends = sum(op[0] == "start" for ops in PLAN for op in ops)
    wide = pltpu.VMEM((TOK, WIDTH), BF)
    return pl.pallas_call(
        kernel,
        out_shape=(out, out),
        in_specs=[hbm] * 7 + [vmem, vmem, pl.BlockSpec(memory_space=pltpu.SMEM)],
        out_specs=(vmem, vmem),
        scratch_shapes=[
            wide, wide, wide, wide, wide,
            pltpu.VMEM((2 * UNITS, 4, TOK, HD), BF),
            pltpu.VMEM((HEADS * TOK, 2 * HD), BF),
            pltpu.VMEM((KEYS, 2 * HD), BF),
            pltpu.VMEM((KEYS, HD), BF),
            pltpu.VMEM((HEADS * TOK, HD), F32),
            pltpu.VMEM((HEADS * TOK, 2 * HD), F32),
            pltpu.VMEM((HEADS, TOK), F32),
            pltpu.VMEM((HEADS, HD, HD), F32),
            pltpu.VMEM((HEADS, 8, HD), F32),
            pltpu.VMEM((TOK, WIDTH), F32),
            pltpu.VMEM((HALF, HD + 16, HD), BF),
            pltpu.VMEM((HALF, HD + 16, HD), BF),
            pltpu.VMEM((NZ, HD + 16, HD), BF),
            pltpu.VMEM((NZ, HD + 16, HD), BF),
            pltpu.VMEM((NZ, HD + 8, HD), F32),
            pltpu.VMEM((HD + 8, HD), F32),
            pltpu.VMEM((NY, HD + 8, HD), F32),
            pltpu.VMEM((NZ, HD, HD), BF),
            pltpu.VMEM((NZ, HD, HD), BF),
            pltpu.VMEM((HALF, HD, HD), BF),
            pltpu.VMEM((HALF, HD, HD), BF),
            pltpu.VMEM((HALF, HD, HD), BF),
            pltpu.VMEM((TOK, HD), F32),
            pltpu.VMEM((4, TOK, HD), F32),
            pltpu.SMEM((2 * UNITS,), jnp.int32),
            pltpu.SemaphoreType.DMA((5,)),
            pltpu.SemaphoreType.DMA((4,)),
            pltpu.SemaphoreType.DMA((len(PART_SIZES) * 2 * UNITS,)),
            pltpu.SemaphoreType.DMA((n_sends,)),
            pltpu.SemaphoreType.DMA((len(PART_SIZES) * UNITS,)),
            pltpu.SemaphoreType.DMA((28,)),
            pltpu.SemaphoreType.DMA((28,)),
        ],
        compiler_params=pltpu.CompilerParams(
            collective_id=0, has_side_effects=True, vmem_limit_bytes=62 * 2**20
        ),
    )(
        q_lin, k_lin, v_lin, gate, queries, keys, values, log_decay, norm_gain.reshape(1, WIDTH), order
    )


def solution(mesh):
    finer = Mesh(
        mesh.devices.reshape(NY, NZ, 2, mesh.shape["head"]), ("y", "z", "c", "x")
    )
    rows = ("y", "z", "c")
    tile = P(rows, "x")
    return jax.shard_map(
        body,
        mesh=finer,
        in_specs=(tile, tile, tile, P("x", rows), tile, P("x"), tile, tile, tile, P(rows)),
        out_specs=(tile, tile),
        check_vma=False,
    )
```

```python
import functools
import math

import jax
import jax.numpy as jnp
from jax import lax
from jax.experimental import pallas as pl
from jax.experimental.pallas import tpu as pltpu
from jax.sharding import Mesh
from jax.sharding import PartitionSpec as P

HD = 128
TOK = 128
HEADS = 16
HALF = 8
WIDTH = HEADS * HD
GROUP = 8
EPS = 1e-06
SCALE2 = math.log2(math.e) / math.sqrt(HD)
NEG = -1e30
MESH = pl.DeviceIdType.MESH
BF = jnp.bfloat16
F32 = jnp.float32
NY, NZ = 4, 8
UNITS = NY * NZ
STEP_UNITS = 2
SHARDS = 2 * STEP_UNITS
KEYS = SHARDS * TOK
STEPS = UNITS // STEP_UNITS
CHUNKS = STEPS


def ring_next(r, size, tie_up):
    r = r % size
    half = size // 2

    def wanted(distance, up):
        return distance < half or (distance == half and up == tie_up)

    if r == 0:
        return [s for s, up in ((-1, True), (1, False)) if wanted(1, up)]
    if r < half or (r == half and tie_up):
        return [-1] if wanted(r + 1, True) else []
    return [1] if wanted(size - r + 1, False) else []


PART_SIZES = (4,)
RATE, LATENCY = 104.0, 1.8
CORE_RATE, CORE_LATENCY = 400.0, 1.1
SOFTMAX, ISSUE, AHEAD_TIME = 1.85, 0.04, 2.0
COST = {"intra": 2.0, "chip_totals": 0.7, "row_scan": 0.7, "prefixes": 0.4, "carries": 0.7, "inter": 1.2, "finish": 0.6}
MESSAGES = {
    "chip_totals": [(("z", 1), 36 * 8), (("z", -1), 36 * 8)],
    "row_scan": [(("y", 1), 70 * 2), (("y", -1), 70 * 2)],
    "prefixes": [(("z", 1), 32 * 8), (("z", -1), 32 * 8)],
    "carries": [(("c", 0), 256)],
    "inter": [(("x", 1), 64 * 2)],
    "finish": [],
}


def sends_of(item):
    part, dy, dz = item
    out = []
    if part == 0:
        if dy == 0:
            out += [("z", s) for s in ring_next(dz, NZ, True)]
        out += [("y", s) for s in ring_next(dy, NY, dz % 2 == 0)]
    else:
        if dz == 0:
            out += [("y", s) for s in ring_next(dy, NY, True)]
        out += [("z", s) for s in ring_next(dz, NZ, dy % 2 == 0)]
    return out


def plan():
    parts = range(len(PART_SIZES))
    free = {}
    arrival = {}
    queues = {(axis, s): [] for axis in "zy" for s in (-1, 1)}
    held, order, chunks, ops = set(), [], [], []
    pending = ["intra"] + list(MESSAGES)
    due = {"intra": 0.0}
    now = 0.0

    def use(way, size):
        rate, latency = (CORE_RATE, CORE_LATENCY) if way[0] == "c" else (RATE / 2, LATENCY)
        free[way] = max(free.get(way, 0.0), now) + size * 1.024 / rate
        return free[way] + latency

    def issue():
        for way, queue in queues.items():
            while queue and free.get(way, 0.0) < now + AHEAD_TIME:
                item = queue.pop(0)
                axis, s = way
                part, dy, dz = item
                target = (part, (dy - s) % NY, dz) if axis == "y" else (part, dy, (dz - s) % NZ)
                arrival[target] = use(way, 32 * PART_SIZES[part])
                ops.append(("start", item, way, target))

    def take(item):
        held.add(item)
        for way in sends_of(item):
            queues[way].append(item)
        issue()
        arrival[item + (1,)] = use(("c", 0), 32 * PART_SIZES[item[0]])
        ops.append(("partner", item))
        if all((p,) + item[1:] in held for p in parts):
            order.append(item[1:])

    due["chip_totals"] = use(("c", 0), 288)
    for p in parts:
        ops.append(("take", (p, 0, 0)))
        take((p, 0, 0))
    done = 0
    while done < CHUNKS or pending:
        while True:
            if pending and due.get(pending[0], 1e9) <= now:
                name = pending.pop(0)
                ops.append(("task", name))
                now += COST[name]
                if pending:
                    sent = [use(way, size) for way, size in MESSAGES.get(name, [])]
                    if sent:
                        due[pending[0]] = max(sent)
                continue
            came = sorted((i for i in arrival if len(i) == 3 and i not in held and arrival[i] <= now), key=lambda i: arrival[i])
            if came:
                now += ISSUE
                ops.append(("take", came[0]))
                take(came[0])
                continue
            break
        issue()
        group = order[done * STEP_UNITS : (done + 1) * STEP_UNITS]
        needs = [(p,) + b + (1,) for b in group for p in parts]
        if done < CHUNKS and len(group) == STEP_UNITS and all(arrival[i] <= now for i in needs):
            chunks.append(ops)
            ops = []
            now += SOFTMAX
            done += 1
            continue
        if done == CHUNKS and not pending:
            break
        later = [arrival[i] for i in arrival if arrival[i] > now]
        if pending and due.get(pending[0], 1e9) > now:
            later.append(due[pending[0]])
        later += [free[w] - AHEAD_TIME + 0.001 for w, q in queues.items() if q and free[w] - AHEAD_TIME > now - 0.001]
        if not later:
            break
        now = max(min(later), now + 1e-6)
    chunks.append(ops)
    return order, chunks


ORDER, PLAN = plan()
UNIT_AT = {block: place for place, block in enumerate(ORDER)}
BOUNDS = [sum(PART_SIZES[:p]) for p in range(len(PART_SIZES) + 1)]


def kernel(
    q_hbm, k_hbm, v_hbm, gate_hbm, queries_hbm, keys_hbm, values_hbm, decay_ref, gain_ref, order_ref,
    mixed_ref, attended_ref,
    qx, kx, vx, gx, qs, buf, qaug, kaug, vaug, top, acc, cum, state, dec, lin,
    s_out, s_in, z_out, z_in, edge, y_out, y_in, p_out, p_in, c_out, carr_a, carr_b, x_out, x_in,
    shard_of, load_sem, kv_load_sem, recv_sem, send_sem, part_sem, small_send, small_recv,
):
    me_y, me_z, me_c, me_x = (lax.axis_index(n) for n in ("y", "z", "c", "x"))
    other = 1 - me_c
    first = me_c == 0

    def at(y=None, z=None, c=None, x=None):
        return (
            me_y if y is None else lax.rem(me_y + y + NY, NY),
            me_z if z is None else lax.rem(me_z + z + NZ, NZ),
            me_c if c is None else other,
            me_x if x is None else lax.rem(me_x + x + 4, 4),
        )

    peers = [at(z=d) for d in range(1, NZ)] + [at(y=d) for d in range(1, NY)]
    peers += [at(x=d) for d in range(1, 4)] + [at(c=1)]

    loads = [
        pltpu.make_async_copy(src, dst, load_sem.at[n])
        for n, (src, dst) in enumerate(
            ((k_hbm, kx), (v_hbm, vx), (q_hbm, qx), (queries_hbm, qs), (gate_hbm, gx))
        )
    ]
    kv_loads = []
    for n, src in enumerate((keys_hbm, values_hbm)):
        for g in range(2):
            kv_loads.append(
                pltpu.make_async_copy(
                    src.at[:, g * HD : (g + 1) * HD], buf.at[0, 2 * n + g], kv_load_sem.at[2 * n + g]
                )
            )
    barrier = pltpu.get_barrier_semaphore()
    for peer in peers:
        pl.semaphore_signal(barrier, inc=1, device_id=peer, device_id_type=MESH)
    for load in kv_loads + loads:
        load.start()

    def remote(src, dst, send, recv, device):
        return pltpu.make_async_remote_copy(
            src_ref=src, dst_ref=dst, send_sem=send, recv_sem=recv, device_id=device, device_id_type=MESH
        )

    send_place = {}
    for ops in PLAN:
        for op in ops:
            if op[0] == "start":
                send_place[op[1:3]] = len(send_place)

    def slot(item, partner):
        return 2 * UNIT_AT[item[1:]] + partner

    def part_of(item, partner):
        return buf.at[slot(item, partner), BOUNDS[item[0]] : BOUNDS[item[0] + 1]]

    def landed(item, partner):
        return recv_sem.at[item[0] * 2 * UNITS + slot(item, partner)]

    def block_copy(item, way, target):
        axis, s = way
        device = at(y=s) if axis == "y" else at(z=s)
        return remote(
            part_of(item, 0), part_of(target, 0), send_sem.at[send_place[(item, way)]], landed(target, 0), device
        )

    def partner_copy(item):
        sem = part_sem.at[item[0] * UNITS + UNIT_AT[item[1:]]]
        return remote(part_of(item, 0), part_of(item, 1), sem, landed(item, 1), at(c=1))

    def arrived(item, partner):
        return remote(part_of(item, partner), part_of(item, partner), part_sem.at[0], landed(item, partner), at(c=1))

    def perform(ops):
        for op in ops:
            if op[0] == "take":
                if op[1][1:] != (0, 0):
                    arrived(op[1], 0).wait_recv()
            elif op[0] == "start":
                block_copy(*op[1:]).start()
            elif op[0] == "partner":
                partner_copy(op[1]).start()
            else:
                tasks[op[1]]()

    x = decay_ref[...]
    lane = lax.broadcasted_iota(jnp.int32, (HEADS, TOK), 1)
    for s in (1, 2, 4, 8, 16, 32, 64):
        x = x + jnp.where(lane >= s, pltpu.roll(x, s, axis=1), 0.0)
    cum[...] = x

    row_i = lax.broadcasted_iota(jnp.int32, (TOK, TOK), 0)
    col_i = lax.broadcasted_iota(jnp.int32, (TOK, TOK), 1)
    lower = row_i >= col_i
    head_rows = lax.broadcasted_iota(jnp.int32, (16, HD), 0)

    def columns(h):
        return pl.ds(pl.multiple_of(h * HD, HD), HD)

    def cum_of(h):
        rows = jnp.broadcast_to(cum[pl.ds(h, 1), :], (TOK, TOK))
        return rows, jnp.transpose(rows)

    def silu(v):
        v = v.astype(F32)
        return (v / (1.0 + jnp.exp(-v))).astype(BF)

    def pack_decay(d):
        hi = d.astype(BF)
        rest = d - hi.astype(F32)
        mid = rest.astype(BF)
        low = (rest - mid.astype(F32)).astype(BF)
        return jnp.where(
            head_rows == 0, hi.astype(F32), jnp.where(head_rows == 1, mid.astype(F32), low.astype(F32))
        ).astype(BF)

    def unpack_decay(rows):
        r = rows.astype(F32)
        return r[0:1] + r[1:2] + r[2:3]

    loads[0].wait()
    loads[1].wait()

    def local_state(h, carry):
        cols = columns(h)
        _, cb = cum_of(h)
        kb = silu(kx[:, cols])
        vb = silu(vx[:, cols])
        kx[:, cols] = kb
        vx[:, cols] = vb
        last = cb[TOK - 1 : TOK, :]
        kdec = (kb.astype(F32) * jnp.exp(last - cb)).astype(BF)
        s = lax.dot_general(kdec, vb, (((0,), (0,)), ((), ())), preferred_element_type=F32)
        state[h] = s
        d = jnp.exp(last)
        dec[h] = jnp.broadcast_to(d, (8, HD))
        return carry

    lax.fori_loop(0, HEADS, local_state, 0, unroll=True)

    def to_partner(r, carry):
        h = other * HALF + r
        s_out[r, 0:HD] = state[h].astype(BF)
        s_out[r, HD : HD + 16] = pack_decay(dec[h][0:1])
        return carry

    lax.fori_loop(0, HALF, to_partner, 0, unroll=True)
    pl.semaphore_wait(barrier, len(peers))
    state_copy = remote(s_out, s_in, small_send.at[0], small_recv.at[0], at(c=1))
    state_copy.start()
    for load in kv_loads:
        load.wait()
    opening = next(n for n, op in enumerate(PLAN[0]) if op[0] == "task")
    perform(PLAN[0][:opening])

    loads[3].wait()
    unit = jnp.where(row_i == col_i, 1.0, 0.0).astype(BF)

    def spread(h, carry):
        rows = pl.ds(pl.multiple_of(h * TOK, TOK), TOK)
        qaug[rows, 0:HD] = qs[:, columns(h)]
        qaug[rows, HD : 2 * HD] = unit
        top[rows, :] = jnp.full((TOK, HD), NEG, F32)
        acc[rows, :] = jnp.zeros((TOK, 2 * HD), F32)
        return carry

    lax.fori_loop(0, HEADS, spread, 0, unroll=True)
    for u, (dy, dz) in enumerate(ORDER):
        chip = lax.rem(me_y + dy, NY) * NZ + lax.rem(me_z + dz, NZ)
        shard_of[2 * u] = 2 * chip + me_c
        shard_of[2 * u + 1] = 2 * chip + other
    my_shard = order_ref[0]
    above = jnp.where(row_i > col_i, NEG, 0.0)

    def softmax(i):
        base = i * SHARDS
        for s in range(SHARDS):
            rows = slice(s * TOK, (s + 1) * TOK)
            shard = shard_of[base + s]
            whole = jnp.where(shard > my_shard, NEG, 0.0)
            part = jnp.where(shard == my_shard, 1.0, 0.0)
            bias = (above * part + whole).astype(BF)
            for g in range(2):
                kaug[g, rows, 0:HD] = buf[base + s, g]
                kaug[g, rows, HD : 2 * HD] = bias
                vaug[g, rows, :] = buf[base + s, 2 + g]
        for g in range(2):
            rows = slice(g * GROUP * TOK, (g + 1) * GROUP * TOK)
            sc = lax.dot_general(
                qaug[rows, :], kaug[g], (((1,), (1,)), ((), ())), preferred_element_type=F32
            )
            old = top[rows, :]
            new = jnp.maximum(old, jnp.max(sc, axis=1, keepdims=True))
            w = jnp.exp2(sc * SCALE2 - jnp.tile(new * SCALE2, (1, SHARDS)))
            alpha = jnp.exp2((old - new) * SCALE2)
            pv = jnp.dot(w.astype(BF), vaug[g], preferred_element_type=F32)
            acc[rows, 0:HD] = acc[rows, 0:HD] * alpha + pv
            den = w[:, 0:HD]
            for s in range(1, SHARDS):
                den = den + w[:, s * HD : (s + 1) * HD]
            acc[rows, HD : 2 * HD] = acc[rows, HD : 2 * HD] * alpha + den
            top[rows, :] = new

    def intra():
        loads[2].wait()

        def one(h, carry):
            cols = columns(h)
            rb, cb = cum_of(h)
            qb = silu(qx[:, cols])
            sc = lax.dot_general(qb, kx[:, cols], (((1,), (1,)), ((), ())), preferred_element_type=F32)
            decay = jnp.where(lower, jnp.exp(jnp.where(lower, cb - rb, 0.0)), 0.0)
            w = (sc * decay).astype(BF)
            lin[:, cols] = jnp.dot(w, vx[:, cols], preferred_element_type=F32)
            qx[:, cols] = (qb.astype(F32) * jnp.exp(cb)).astype(BF)
            return carry

        lax.fori_loop(0, HEADS, one, 0, unroll=True)

    def z_copy(d):
        head = lax.rem(me_z + d, NZ)
        return remote(z_out.at[head], z_in.at[NZ - d], small_send.at[d], small_recv.at[NZ - d], at(z=d))

    def z_arrival(d):
        return remote(z_out.at[0], z_in.at[d], small_send.at[0], small_recv.at[d], at(z=d))

    def chip_totals():
        remote(s_out, s_in, small_send.at[0], small_recv.at[0], at(c=1)).wait_recv()

        def one(r, carry):
            h = me_c * HALF + r
            mine, d_mine = state[h], dec[h][0:1]
            theirs = s_in[r, 0:HD].astype(F32)
            d_theirs = unpack_decay(s_in[r, HD : HD + 16])
            total = jnp.where(first, d_theirs, 1.0) * mine + jnp.where(first, 1.0, d_mine) * theirs
            z_out[r, 0:HD] = total.astype(BF)
            z_out[r, HD : HD + 16] = pack_decay(d_mine * d_theirs)
            return carry

        lax.fori_loop(0, HALF, one, 0, unroll=True)
        for d in range(1, NZ):
            z_copy(d).start()

    def y_copy(d):
        return remote(y_out, y_in.at[NY - d], small_send.at[8 + d], small_recv.at[8 + NY - d], at(y=d))

    def y_arrival(d):
        return remote(y_out, y_in.at[d], small_send.at[0], small_recv.at[8 + d], at(y=d))

    def row_scan():
        for d in range(1, NZ):
            z_arrival(d).wait_recv()
        z_in[0] = z_out[me_z]

        def one(k, carry):
            e, a = carry
            rel = lax.rem(k - me_z + NZ, NZ)
            edge[k, 0:HD] = e
            edge[k, HD : HD + 8] = jnp.broadcast_to(a, (8, HD))
            d = unpack_decay(z_in[rel, HD : HD + 16])
            return d * e + z_in[rel, 0:HD].astype(F32), a * d

        e, a = lax.fori_loop(0, NZ, one, (jnp.zeros((HD, HD), F32), jnp.ones((1, HD), F32)))
        y_out[0:HD] = e
        y_out[HD : HD + 8] = jnp.broadcast_to(a, (8, HD))
        y_in[0] = jnp.zeros((HD + 8, HD), F32)
        for d in range(1, NY):
            y_copy(d).start()

    def p_copy(d):
        chip = lax.rem(me_z + d, NZ)
        return remote(p_out.at[chip], p_in.at[NZ - d], small_send.at[16 + d], small_recv.at[16 + NZ - d], at(z=d))

    def p_arrival(d):
        return remote(p_out.at[0], p_in.at[d], small_send.at[0], small_recv.at[16 + d], at(z=d))

    def prefixes():
        for d in range(1, NY):
            y_arrival(d).wait_recv()
        carry = jnp.zeros((HD, HD), F32)
        for k in range(NY - 1):
            rel = lax.rem(k - me_y + NY, NY)
            grown = y_in[rel, HD : HD + 1] * carry + y_in[rel, 0:HD]
            carry = jnp.where(k < me_y, grown, carry)

        for k in range(NZ):
            p_out[k] = (edge[k, 0:HD] + edge[k, HD : HD + 1] * carry).astype(BF)
        for d in range(1, NZ):
            p_copy(d).start()

    def carries():
        for d in range(1, NZ):
            p_arrival(d).wait_recv()
        p_in[0] = p_out[me_z]

        def one(r, carry):
            h = me_c * HALF + r
            before = p_in[lax.rem(r - me_z + NZ, NZ)].astype(F32)
            d_theirs = unpack_decay(s_in[r, HD : HD + 16])
            d = jnp.where(first, dec[h][0:1], d_theirs)
            s = jnp.where(first, state[h], s_in[r, 0:HD].astype(F32))
            after = d * before + s
            carr_a[r] = jnp.where(first, before, after).astype(BF)
            c_out[r] = jnp.where(first, after, before).astype(BF)
            return carry

        lax.fori_loop(0, HALF, one, 0, unroll=True)
        remote(c_out, carr_b, small_send.at[24], small_recv.at[24], at(c=1)).start()

    def x_copy(d):
        return remote(x_out, x_in.at[4 - d], small_send.at[24 + d], small_recv.at[24 + 4 - d], at(x=d))

    def x_arrival(d):
        return remote(x_out, x_in.at[d], small_send.at[0], small_recv.at[24 + d], at(x=d))

    def inter():
        def half(source, start):
            def one(r, total):
                cols = columns(start + r)
                value = lin[:, cols] + jnp.dot(qx[:, cols], source[r], preferred_element_type=F32)
                lin[:, cols] = value
                return total + value * value

            return one

        total = lax.fori_loop(
            0, HALF, half(carr_a, me_c * HALF), jnp.zeros((TOK, HD), F32), unroll=True
        )
        remote(c_out, carr_b, small_send.at[24], small_recv.at[24], at(c=1)).wait_recv()
        total = lax.fori_loop(0, HALF, half(carr_b, other * HALF), total, unroll=True)
        x_out[...] = total
        for d in range(1, 4):
            x_copy(d).start()

    def finish():
        loads[4].wait()
        total = x_out[...]
        for d in range(1, 4):
            x_arrival(d).wait_recv()
            total = total + x_in[d]
        inv = lax.rsqrt(jnp.sum(total, axis=1, keepdims=True) / (4 * WIDTH) + EPS)
        inv = jnp.broadcast_to(inv, (TOK, HD))

        def one(h, carry):
            cols = columns(h)
            g = gx[:, cols].astype(F32)
            gated = 1.0 / (1.0 + jnp.exp(-g))
            mixed_ref[:, cols] = (lin[:, cols] * inv * gain_ref[:, cols] * gated).astype(BF)
            return carry

        lax.fori_loop(0, HEADS, one, 0, unroll=True)

    tasks = {
        task.__name__: task for task in (intra, chip_totals, row_scan, prefixes, carries, inter, finish)
    }

    def chunk(i, carry):
        for c in range(CHUNKS):

            @pl.when(i == c)
            def _(c=c):
                perform(PLAN[c][opening:] if c == 0 else PLAN[c])
                for u in range(c * STEP_UNITS, (c + 1) * STEP_UNITS):
                    for part in range(len(PART_SIZES)):
                        arrived((part,) + ORDER[u], 1).wait_recv()

        softmax(i)
        return carry

    lax.fori_loop(0, CHUNKS, chunk, 0)
    perform(PLAN[CHUNKS])

    def result(h, carry):
        rows = pl.ds(pl.multiple_of(h * TOK, TOK), TOK)
        den = jnp.sum(acc[rows, HD : 2 * HD], axis=1, keepdims=True)
        attended_ref[:, columns(h)] = (acc[rows, 0:HD] / den).astype(BF)
        return carry

    lax.fori_loop(0, HEADS, result, 0, unroll=True)

    state_copy.wait_send()
    for d in range(1, NZ):
        z_copy(d).wait_send()
        p_copy(d).wait_send()
    for d in range(1, NY):
        y_copy(d).wait_send()
    remote(c_out, carr_b, small_send.at[24], small_recv.at[24], at(c=1)).wait_send()
    for d in range(1, 4):
        x_copy(d).wait_send()
    for ops in PLAN:
        for op in ops:
            if op[0] == "start":
                block_copy(*op[1:]).wait_send()
            elif op[0] == "partner":
                partner_copy(op[1]).wait_send()


def hand_over(a_ref, b_ref, a_out, b_out):
    a_out[...] = a_ref[...]
    b_out[...] = b_ref[...]


def body(q_lin, k_lin, v_lin, log_decay, gate, norm_gain, queries, keys, values, order):
    vmem = pl.BlockSpec(memory_space=pltpu.VMEM)
    hbm = pl.BlockSpec(memory_space=pl.ANY)
    out = jax.ShapeDtypeStruct((TOK, WIDTH), BF)
    n_sends = sum(op[0] == "start" for ops in PLAN for op in ops)
    wide = pltpu.VMEM((TOK, WIDTH), BF)
    mixed, attended = pl.pallas_call(
        kernel,
        out_shape=(out, out),
        in_specs=[hbm] * 7 + [vmem, vmem, pl.BlockSpec(memory_space=pltpu.SMEM)],
        out_specs=(vmem, vmem),
        scratch_shapes=[
            wide, wide, wide, wide, wide,
            pltpu.VMEM((2 * UNITS, 4, TOK, HD), BF),
            pltpu.VMEM((HEADS * TOK, 2 * HD), BF),
            pltpu.VMEM((2, KEYS, 2 * HD), BF),
            pltpu.VMEM((2, KEYS, HD), BF),
            pltpu.VMEM((HEADS * TOK, HD), F32),
            pltpu.VMEM((HEADS * TOK, 2 * HD), F32),
            pltpu.VMEM((HEADS, TOK), F32),
            pltpu.VMEM((HEADS, HD, HD), F32),
            pltpu.VMEM((HEADS, 8, HD), F32),
            pltpu.VMEM((TOK, WIDTH), F32),
            pltpu.VMEM((HALF, HD + 16, HD), BF),
            pltpu.VMEM((HALF, HD + 16, HD), BF),
            pltpu.VMEM((NZ, HD + 16, HD), BF),
            pltpu.VMEM((NZ, HD + 16, HD), BF),
            pltpu.VMEM((NZ, HD + 8, HD), F32),
            pltpu.VMEM((HD + 8, HD), F32),
            pltpu.VMEM((NY, HD + 8, HD), F32),
            pltpu.VMEM((NZ, HD, HD), BF),
            pltpu.VMEM((NZ, HD, HD), BF),
            pltpu.VMEM((HALF, HD, HD), BF),
            pltpu.VMEM((HALF, HD, HD), BF),
            pltpu.VMEM((HALF, HD, HD), BF),
            pltpu.VMEM((TOK, HD), F32),
            pltpu.VMEM((4, TOK, HD), F32),
            pltpu.SMEM((2 * UNITS,), jnp.int32),
            pltpu.SemaphoreType.DMA((5,)),
            pltpu.SemaphoreType.DMA((4,)),
            pltpu.SemaphoreType.DMA((len(PART_SIZES) * 2 * UNITS,)),
            pltpu.SemaphoreType.DMA((n_sends,)),
            pltpu.SemaphoreType.DMA((len(PART_SIZES) * UNITS,)),
            pltpu.SemaphoreType.DMA((28,)),
            pltpu.SemaphoreType.DMA((28,)),
        ],
        compiler_params=pltpu.CompilerParams(
            collective_id=0, has_side_effects=True, vmem_limit_bytes=62 * 2**20
        ),
    )(
        q_lin, k_lin, v_lin, gate, queries, keys, values, log_decay, norm_gain.reshape(1, WIDTH), order
    )
    block = pl.BlockSpec((TOK // 4, WIDTH), lambda i: (i, 0))
    return pl.pallas_call(
        hand_over, grid=(4,), out_shape=(out, out), in_specs=[block, block], out_specs=(block, block)
    )(mixed, attended)


def solution(mesh):
    finer = Mesh(
        mesh.devices.reshape(NY, NZ, 2, mesh.shape["head"]), ("y", "z", "c", "x")
    )
    rows = ("y", "z", "c")
    tile = P(rows, "x")
    return jax.shard_map(
        body,
        mesh=finer,
        in_specs=(tile, tile, tile, P("x", rows), tile, P("x"), tile, tile, tile, P(rows)),
        out_specs=(tile, tile),
        check_vma=False,
    )
```

```python
import functools
import math

import jax
import jax.numpy as jnp
from jax import lax
from jax.experimental import pallas as pl
from jax.experimental.pallas import tpu as pltpu
from jax.sharding import Mesh
from jax.sharding import PartitionSpec as P

HD = 128
TOK = 128
HEADS = 16
HALF = 8
WIDTH = HEADS * HD
GROUP = 8
EPS = 1e-06
SCALE2 = math.log2(math.e) / math.sqrt(HD)
NEG = -1e30
MESH = pl.DeviceIdType.MESH
BF = jnp.bfloat16
F32 = jnp.float32
NY, NZ = 4, 8
UNITS = NY * NZ
STEP_UNITS = 2
SHARDS = 2 * STEP_UNITS
KEYS = SHARDS * TOK
STEPS = UNITS // STEP_UNITS
CHUNKS = STEPS


def ring_next(r, size, tie_up):
    r = r % size
    half = size // 2

    def wanted(distance, up):
        return distance < half or (distance == half and up == tie_up)

    if r == 0:
        return [s for s, up in ((-1, True), (1, False)) if wanted(1, up)]
    if r < half or (r == half and tie_up):
        return [-1] if wanted(r + 1, True) else []
    return [1] if wanted(size - r + 1, False) else []


PART_SIZES = (4,)
RATE, LATENCY = 104.0, 1.8
CORE_RATE, CORE_LATENCY = 400.0, 1.1
SOFTMAX, ISSUE, AHEAD_TIME = 1.85, 0.04, 2.0
COST = {"intra": 2.0, "chip_totals": 0.7, "row_scan": 0.7, "prefixes": 0.4, "carries": 0.7, "inter": 1.2, "finish": 0.6}
MESSAGES = {
    "chip_totals": [(("z", 1), 36 * 8), (("z", -1), 36 * 8)],
    "row_scan": [(("y", 1), 70 * 2), (("y", -1), 70 * 2)],
    "prefixes": [(("z", 1), 32 * 8), (("z", -1), 32 * 8)],
    "carries": [(("c", 0), 256)],
    "inter": [(("x", 1), 64 * 2)],
    "finish": [],
}


def sends_of(item):
    part, dy, dz = item
    out = []
    if part == 0:
        if dy == 0:
            out += [("z", s) for s in ring_next(dz, NZ, True)]
        out += [("y", s) for s in ring_next(dy, NY, dz % 2 == 0)]
    else:
        if dz == 0:
            out += [("y", s) for s in ring_next(dy, NY, True)]
        out += [("z", s) for s in ring_next(dz, NZ, dy % 2 == 0)]
    return out


def plan():
    parts = range(len(PART_SIZES))
    free = {}
    arrival = {}
    queues = {(axis, s): [] for axis in "zy" for s in (-1, 1)}
    held, order, chunks, ops = set(), [], [], []
    pending = ["intra"] + list(MESSAGES)
    due = {"intra": 0.0}
    now = 0.0

    def use(way, size):
        rate, latency = (CORE_RATE, CORE_LATENCY) if way[0] == "c" else (RATE / 2, LATENCY)
        free[way] = max(free.get(way, 0.0), now) + size * 1.024 / rate
        return free[way] + latency

    def issue():
        for way, queue in queues.items():
            while queue and free.get(way, 0.0) < now + AHEAD_TIME:
                item = queue.pop(0)
                axis, s = way
                part, dy, dz = item
                target = (part, (dy - s) % NY, dz) if axis == "y" else (part, dy, (dz - s) % NZ)
                arrival[target] = use(way, 32 * PART_SIZES[part])
                ops.append(("start", item, way, target))

    def take(item):
        held.add(item)
        for way in sends_of(item):
            queues[way].append(item)
        issue()
        arrival[item + (1,)] = use(("c", 0), 32 * PART_SIZES[item[0]])
        ops.append(("partner", item))
        if all((p,) + item[1:] in held for p in parts):
            order.append(item[1:])

    due["chip_totals"] = use(("c", 0), 288)
    for p in parts:
        ops.append(("take", (p, 0, 0)))
        take((p, 0, 0))
    done = 0
    while done < CHUNKS or pending:
        while True:
            if pending and due.get(pending[0], 1e9) <= now:
                name = pending.pop(0)
                ops.append(("task", name))
                now += COST[name]
                if pending:
                    sent = [use(way, size) for way, size in MESSAGES.get(name, [])]
                    if sent:
                        due[pending[0]] = max(sent)
                continue
            came = sorted((i for i in arrival if len(i) == 3 and i not in held and arrival[i] <= now), key=lambda i: arrival[i])
            if came:
                now += ISSUE
                ops.append(("take", came[0]))
                take(came[0])
                continue
            break
        issue()
        group = order[done * STEP_UNITS : (done + 1) * STEP_UNITS]
        needs = [(p,) + b + (1,) for b in group for p in parts]
        if done < CHUNKS and len(group) == STEP_UNITS and all(arrival[i] <= now for i in needs):
            chunks.append(ops)
            ops = []
            now += SOFTMAX
            done += 1
            continue
        if done == CHUNKS and not pending:
            break
        later = [arrival[i] for i in arrival if arrival[i] > now]
        if pending and due.get(pending[0], 1e9) > now:
            later.append(due[pending[0]])
        later += [free[w] - AHEAD_TIME + 0.001 for w, q in queues.items() if q and free[w] - AHEAD_TIME > now - 0.001]
        if not later:
            break
        now = max(min(later), now + 1e-6)
    chunks.append(ops)
    return order, chunks


ORDER, PLAN = plan()
UNIT_AT = {block: place for place, block in enumerate(ORDER)}
BOUNDS = [sum(PART_SIZES[:p]) for p in range(len(PART_SIZES) + 1)]


def kernel(
    q_hbm, k_hbm, v_hbm, gate_hbm, queries_hbm, keys_hbm, values_hbm, decay_ref, gain_ref, order_ref,
    mixed_ref, attended_ref,
    qx, kx, vx, gx, qs, buf, qaug, kaug, vaug, top, acc, cum, state, dec, lin,
    s_out, s_in, z_out, z_in, edge, y_out, y_in, p_out, p_in, c_out, carr_a, carr_b, x_out, x_in,
    shard_of, load_sem, kv_load_sem, recv_sem, send_sem, part_sem, small_send, small_recv,
):
    me_y, me_z, me_c, me_x = (lax.axis_index(n) for n in ("y", "z", "c", "x"))
    other = 1 - me_c
    first = me_c == 0

    def at(y=None, z=None, c=None, x=None):
        return (
            me_y if y is None else lax.rem(me_y + y + NY, NY),
            me_z if z is None else lax.rem(me_z + z + NZ, NZ),
            me_c if c is None else other,
            me_x if x is None else lax.rem(me_x + x + 4, 4),
        )

    peers = [at(z=d) for d in range(1, NZ)] + [at(y=d) for d in range(1, NY)]
    peers += [at(x=d) for d in range(1, 4)] + [at(c=1)]

    loads = [
        pltpu.make_async_copy(src, dst, load_sem.at[n])
        for n, (src, dst) in enumerate(
            ((k_hbm, kx), (v_hbm, vx), (q_hbm, qx), (queries_hbm, qs), (gate_hbm, gx))
        )
    ]
    kv_loads = []
    for n, src in enumerate((keys_hbm, values_hbm)):
        for g in range(2):
            kv_loads.append(
                pltpu.make_async_copy(
                    src.at[:, g * HD : (g + 1) * HD], buf.at[0, 2 * n + g], kv_load_sem.at[2 * n + g]
                )
            )
    barrier = pltpu.get_barrier_semaphore()
    for peer in peers:
        pl.semaphore_signal(barrier, inc=1, device_id=peer, device_id_type=MESH)
    for load in kv_loads + loads:
        load.start()

    def remote(src, dst, send, recv, device):
        return pltpu.make_async_remote_copy(
            src_ref=src, dst_ref=dst, send_sem=send, recv_sem=recv, device_id=device, device_id_type=MESH
        )

    send_place = {}
    for ops in PLAN:
        for op in ops:
            if op[0] == "start":
                send_place[op[1:3]] = len(send_place)

    def slot(item, partner):
        return 2 * UNIT_AT[item[1:]] + partner

    def part_of(item, partner):
        return buf.at[slot(item, partner), BOUNDS[item[0]] : BOUNDS[item[0] + 1]]

    def landed(item, partner):
        return recv_sem.at[item[0] * 2 * UNITS + slot(item, partner)]

    def block_copy(item, way, target):
        axis, s = way
        device = at(y=s) if axis == "y" else at(z=s)
        return remote(
            part_of(item, 0), part_of(target, 0), send_sem.at[send_place[(item, way)]], landed(target, 0), device
        )

    def partner_copy(item):
        sem = part_sem.at[item[0] * UNITS + UNIT_AT[item[1:]]]
        return remote(part_of(item, 0), part_of(item, 1), sem, landed(item, 1), at(c=1))

    def arrived(item, partner):
        return remote(part_of(item, partner), part_of(item, partner), part_sem.at[0], landed(item, partner), at(c=1))

    def perform(ops):
        for op in ops:
            if op[0] == "take":
                if op[1][1:] != (0, 0):
                    arrived(op[1], 0).wait_recv()
            elif op[0] == "start":
                block_copy(*op[1:]).start()
            elif op[0] == "partner":
                partner_copy(op[1]).start()
            else:
                tasks[op[1]]()

    x = decay_ref[...]
    lane = lax.broadcasted_iota(jnp.int32, (HEADS, TOK), 1)
    for s in (1, 2, 4, 8, 16, 32, 64):
        x = x + jnp.where(lane >= s, pltpu.roll(x, s, axis=1), 0.0)
    cum[...] = x

    row_i = lax.broadcasted_iota(jnp.int32, (TOK, TOK), 0)
    col_i = lax.broadcasted_iota(jnp.int32, (TOK, TOK), 1)
    lower = row_i >= col_i
    head_rows = lax.broadcasted_iota(jnp.int32, (16, HD), 0)

    def columns(h):
        return pl.ds(pl.multiple_of(h * HD, HD), HD)

    def cum_of(h):
        rows = jnp.broadcast_to(cum[pl.ds(h, 1), :], (TOK, TOK))
        return rows, jnp.transpose(rows)

    def silu(v):
        v = v.astype(F32)
        return (v / (1.0 + jnp.exp(-v))).astype(BF)

    def pack_decay(d):
        hi = d.astype(BF)
        rest = d - hi.astype(F32)
        mid = rest.astype(BF)
        low = (rest - mid.astype(F32)).astype(BF)
        return jnp.where(
            head_rows == 0, hi.astype(F32), jnp.where(head_rows == 1, mid.astype(F32), low.astype(F32))
        ).astype(BF)

    def unpack_decay(rows):
        r = rows.astype(F32)
        return r[0:1] + r[1:2] + r[2:3]

    loads[0].wait()
    loads[1].wait()

    def local_state(h, carry):
        cols = columns(h)
        _, cb = cum_of(h)
        kb = silu(kx[:, cols])
        vb = silu(vx[:, cols])
        kx[:, cols] = kb
        vx[:, cols] = vb
        last = cb[TOK - 1 : TOK, :]
        kdec = (kb.astype(F32) * jnp.exp(last - cb)).astype(BF)
        s = lax.dot_general(kdec, vb, (((0,), (0,)), ((), ())), preferred_element_type=F32)
        state[h] = s
        d = jnp.exp(last)
        dec[h] = jnp.broadcast_to(d, (8, HD))
        return carry

    lax.fori_loop(0, HEADS, local_state, 0, unroll=True)

    def to_partner(r, carry):
        h = other * HALF + r
        s_out[r, 0:HD] = state[h].astype(BF)
        s_out[r, HD : HD + 16] = pack_decay(dec[h][0:1])
        return carry

    lax.fori_loop(0, HALF, to_partner, 0, unroll=True)
    loads[3].wait()
    unit = jnp.where(row_i == col_i, 1.0, 0.0).astype(BF)

    def spread(h, carry):
        rows = pl.ds(pl.multiple_of(h * TOK, TOK), TOK)
        qaug[rows, 0:HD] = qs[:, columns(h)]
        qaug[rows, HD : 2 * HD] = unit
        top[rows, :] = jnp.full((TOK, HD), NEG, F32)
        acc[rows, :] = jnp.zeros((TOK, 2 * HD), F32)
        return carry

    lax.fori_loop(0, HEADS, spread, 0, unroll=True)
    for u, (dy, dz) in enumerate(ORDER):
        chip = lax.rem(me_y + dy, NY) * NZ + lax.rem(me_z + dz, NZ)
        shard_of[2 * u] = 2 * chip + me_c
        shard_of[2 * u + 1] = 2 * chip + other
    my_shard = order_ref[0]
    above = jnp.where(row_i > col_i, NEG, 0.0)

    pl.semaphore_wait(barrier, len(peers))
    state_copy = remote(s_out, s_in, small_send.at[0], small_recv.at[0], at(c=1))
    state_copy.start()
    for load in kv_loads:
        load.wait()
    opening = next(n for n, op in enumerate(PLAN[0]) if op[0] == "task")
    perform(PLAN[0][:opening])

    def softmax(i):
        base = i * SHARDS
        for s in range(SHARDS):
            rows = slice(s * TOK, (s + 1) * TOK)
            shard = shard_of[base + s]
            whole = jnp.where(shard > my_shard, NEG, 0.0)
            part = jnp.where(shard == my_shard, 1.0, 0.0)
            bias = (above * part + whole).astype(BF)
            for g in range(2):
                kaug[g, rows, 0:HD] = buf[base + s, g]
                kaug[g, rows, HD : 2 * HD] = bias
                vaug[g, rows, :] = buf[base + s, 2 + g]
        for g in range(2):
            rows = slice(g * GROUP * TOK, (g + 1) * GROUP * TOK)
            sc = lax.dot_general(
                qaug[rows, :], kaug[g], (((1,), (1,)), ((), ())), preferred_element_type=F32
            )
            old = top[rows, :]
            new = jnp.maximum(old, jnp.max(sc, axis=1, keepdims=True))
            w = jnp.exp2(sc * SCALE2 - jnp.tile(new * SCALE2, (1, SHARDS)))
            alpha = jnp.exp2((old - new) * SCALE2)
            pv = jnp.dot(w.astype(BF), vaug[g], preferred_element_type=F32)
            acc[rows, 0:HD] = acc[rows, 0:HD] * alpha + pv
            den = w[:, 0:HD]
            for s in range(1, SHARDS):
                den = den + w[:, s * HD : (s + 1) * HD]
            acc[rows, HD : 2 * HD] = acc[rows, HD : 2 * HD] * alpha + den
            top[rows, :] = new

    def intra():
        loads[2].wait()

        def one(h, carry):
            cols = columns(h)
            rb, cb = cum_of(h)
            qb = silu(qx[:, cols])
            sc = lax.dot_general(qb, kx[:, cols], (((1,), (1,)), ((), ())), preferred_element_type=F32)
            decay = jnp.where(lower, jnp.exp(jnp.where(lower, cb - rb, 0.0)), 0.0)
            w = (sc * decay).astype(BF)
            lin[:, cols] = jnp.dot(w, vx[:, cols], preferred_element_type=F32)
            qx[:, cols] = (qb.astype(F32) * jnp.exp(cb)).astype(BF)
            return carry

        lax.fori_loop(0, HEADS, one, 0, unroll=True)

    def z_copy(d):
        head = lax.rem(me_z + d, NZ)
        return remote(z_out.at[head], z_in.at[NZ - d], small_send.at[d], small_recv.at[NZ - d], at(z=d))

    def z_arrival(d):
        return remote(z_out.at[0], z_in.at[d], small_send.at[0], small_recv.at[d], at(z=d))

    def chip_totals():
        remote(s_out, s_in, small_send.at[0], small_recv.at[0], at(c=1)).wait_recv()

        def one(r, carry):
            h = me_c * HALF + r
            mine, d_mine = state[h], dec[h][0:1]
            theirs = s_in[r, 0:HD].astype(F32)
            d_theirs = unpack_decay(s_in[r, HD : HD + 16])
            total = jnp.where(first, d_theirs, 1.0) * mine + jnp.where(first, 1.0, d_mine) * theirs
            z_out[r, 0:HD] = total.astype(BF)
            z_out[r, HD : HD + 16] = pack_decay(d_mine * d_theirs)
            return carry

        lax.fori_loop(0, HALF, one, 0, unroll=True)
        for d in range(1, NZ):
            z_copy(d).start()

    def y_copy(d):
        return remote(y_out, y_in.at[NY - d], small_send.at[8 + d], small_recv.at[8 + NY - d], at(y=d))

    def y_arrival(d):
        return remote(y_out, y_in.at[d], small_send.at[0], small_recv.at[8 + d], at(y=d))

    def row_scan():
        for d in range(1, NZ):
            z_arrival(d).wait_recv()
        z_in[0] = z_out[me_z]

        def one(k, carry):
            e, a = carry
            rel = lax.rem(k - me_z + NZ, NZ)
            edge[k, 0:HD] = e
            edge[k, HD : HD + 8] = jnp.broadcast_to(a, (8, HD))
            d = unpack_decay(z_in[rel, HD : HD + 16])
            return d * e + z_in[rel, 0:HD].astype(F32), a * d

        e, a = lax.fori_loop(0, NZ, one, (jnp.zeros((HD, HD), F32), jnp.ones((1, HD), F32)))
        y_out[0:HD] = e
        y_out[HD : HD + 8] = jnp.broadcast_to(a, (8, HD))
        y_in[0] = jnp.zeros((HD + 8, HD), F32)
        for d in range(1, NY):
            y_copy(d).start()

    def p_copy(d):
        chip = lax.rem(me_z + d, NZ)
        return remote(p_out.at[chip], p_in.at[NZ - d], small_send.at[16 + d], small_recv.at[16 + NZ - d], at(z=d))

    def p_arrival(d):
        return remote(p_out.at[0], p_in.at[d], small_send.at[0], small_recv.at[16 + d], at(z=d))

    def prefixes():
        for d in range(1, NY):
            y_arrival(d).wait_recv()
        carry = jnp.zeros((HD, HD), F32)
        for k in range(NY - 1):
            rel = lax.rem(k - me_y + NY, NY)
            grown = y_in[rel, HD : HD + 1] * carry + y_in[rel, 0:HD]
            carry = jnp.where(k < me_y, grown, carry)

        for k in range(NZ):
            p_out[k] = (edge[k, 0:HD] + edge[k, HD : HD + 1] * carry).astype(BF)
        for d in range(1, NZ):
            p_copy(d).start()

    def carries():
        for d in range(1, NZ):
            p_arrival(d).wait_recv()
        p_in[0] = p_out[me_z]

        def one(r, carry):
            h = me_c * HALF + r
            before = p_in[lax.rem(r - me_z + NZ, NZ)].astype(F32)
            d_theirs = unpack_decay(s_in[r, HD : HD + 16])
            d = jnp.where(first, dec[h][0:1], d_theirs)
            s = jnp.where(first, state[h], s_in[r, 0:HD].astype(F32))
            after = d * before + s
            carr_a[r] = jnp.where(first, before, after).astype(BF)
            c_out[r] = jnp.where(first, after, before).astype(BF)
            return carry

        lax.fori_loop(0, HALF, one, 0, unroll=True)
        remote(c_out, carr_b, small_send.at[24], small_recv.at[24], at(c=1)).start()

    def x_copy(d):
        return remote(x_out, x_in.at[4 - d], small_send.at[24 + d], small_recv.at[24 + 4 - d], at(x=d))

    def x_arrival(d):
        return remote(x_out, x_in.at[d], small_send.at[0], small_recv.at[24 + d], at(x=d))

    def inter():
        def half(source, start):
            def one(r, total):
                cols = columns(start + r)
                value = lin[:, cols] + jnp.dot(qx[:, cols], source[r], preferred_element_type=F32)
                lin[:, cols] = value
                return total + value * value

            return one

        total = lax.fori_loop(
            0, HALF, half(carr_a, me_c * HALF), jnp.zeros((TOK, HD), F32), unroll=True
        )
        remote(c_out, carr_b, small_send.at[24], small_recv.at[24], at(c=1)).wait_recv()
        total = lax.fori_loop(0, HALF, half(carr_b, other * HALF), total, unroll=True)
        x_out[...] = total
        for d in range(1, 4):
            x_copy(d).start()

    def finish():
        loads[4].wait()
        total = x_out[...]
        for d in range(1, 4):
            x_arrival(d).wait_recv()
            total = total + x_in[d]
        inv = lax.rsqrt(jnp.sum(total, axis=1, keepdims=True) / (4 * WIDTH) + EPS)
        inv = jnp.broadcast_to(inv, (TOK, HD))

        def one(h, carry):
            cols = columns(h)
            g = gx[:, cols].astype(F32)
            gated = 1.0 / (1.0 + jnp.exp(-g))
            mixed_ref[:, cols] = (lin[:, cols] * inv * gain_ref[:, cols] * gated).astype(BF)
            return carry

        lax.fori_loop(0, HEADS, one, 0, unroll=True)

    tasks = {
        task.__name__: task for task in (intra, chip_totals, row_scan, prefixes, carries, inter, finish)
    }

    def chunk(i, carry):
        for c in range(CHUNKS):

            @pl.when(i == c)
            def _(c=c):
                perform(PLAN[c][opening:] if c == 0 else PLAN[c])
                for u in range(c * STEP_UNITS, (c + 1) * STEP_UNITS):
                    for part in range(len(PART_SIZES)):
                        arrived((part,) + ORDER[u], 1).wait_recv()

        softmax(i)
        return carry

    lax.fori_loop(0, CHUNKS, chunk, 0)
    perform(PLAN[CHUNKS])

    def result(h, carry):
        rows = pl.ds(pl.multiple_of(h * TOK, TOK), TOK)
        den = jnp.sum(acc[rows, HD : 2 * HD], axis=1, keepdims=True)
        attended_ref[:, columns(h)] = (acc[rows, 0:HD] / den).astype(BF)
        return carry

    lax.fori_loop(0, HEADS, result, 0, unroll=True)

    state_copy.wait_send()
    for d in range(1, NZ):
        z_copy(d).wait_send()
        p_copy(d).wait_send()
    for d in range(1, NY):
        y_copy(d).wait_send()
    remote(c_out, carr_b, small_send.at[24], small_recv.at[24], at(c=1)).wait_send()
    for d in range(1, 4):
        x_copy(d).wait_send()
    for ops in PLAN:
        for op in ops:
            if op[0] == "start":
                block_copy(*op[1:]).wait_send()
            elif op[0] == "partner":
                partner_copy(op[1]).wait_send()


def hand_over(a_ref, b_ref, a_out, b_out, held, in_sem, out_sem):
    pieces = [(n, r) for n in range(2) for r in range(2)]
    rows = [slice(r * TOK // 2, (r + 1) * TOK // 2) for r in range(2)]
    loads = [
        pltpu.make_async_copy((a_ref, b_ref)[n].at[rows[r]], held.at[n, rows[r]], in_sem.at[2 * n + r])
        for n, r in pieces
    ]
    stores = [
        pltpu.make_async_copy(held.at[n, rows[r]], (a_out, b_out)[n].at[rows[r]], out_sem.at[2 * n + r])
        for n, r in pieces
    ]
    for load in loads:
        load.start()
    for load, store in zip(loads, stores):
        load.wait()
        store.start()
    for store in stores:
        store.wait()


def body(q_lin, k_lin, v_lin, log_decay, gate, norm_gain, queries, keys, values, order):
    vmem = pl.BlockSpec(memory_space=pltpu.VMEM)
    hbm = pl.BlockSpec(memory_space=pl.ANY)
    out = jax.ShapeDtypeStruct((TOK, WIDTH), BF)
    n_sends = sum(op[0] == "start" for ops in PLAN for op in ops)
    wide = pltpu.VMEM((TOK, WIDTH), BF)
    mixed, attended = pl.pallas_call(
        kernel,
        out_shape=(out, out),
        in_specs=[hbm] * 7 + [vmem, vmem, pl.BlockSpec(memory_space=pltpu.SMEM)],
        out_specs=(vmem, vmem),
        scratch_shapes=[
            wide, wide, wide, wide, wide,
            pltpu.VMEM((2 * UNITS, 4, TOK, HD), BF),
            pltpu.VMEM((HEADS * TOK, 2 * HD), BF),
            pltpu.VMEM((2, KEYS, 2 * HD), BF),
            pltpu.VMEM((2, KEYS, HD), BF),
            pltpu.VMEM((HEADS * TOK, HD), F32),
            pltpu.VMEM((HEADS * TOK, 2 * HD), F32),
            pltpu.VMEM((HEADS, TOK), F32),
            pltpu.VMEM((HEADS, HD, HD), F32),
            pltpu.VMEM((HEADS, 8, HD), F32),
            pltpu.VMEM((TOK, WIDTH), F32),
            pltpu.VMEM((HALF, HD + 16, HD), BF),
            pltpu.VMEM((HALF, HD + 16, HD), BF),
            pltpu.VMEM((NZ, HD + 16, HD), BF),
            pltpu.VMEM((NZ, HD + 16, HD), BF),
            pltpu.VMEM((NZ, HD + 8, HD), F32),
            pltpu.VMEM((HD + 8, HD), F32),
            pltpu.VMEM((NY, HD + 8, HD), F32),
            pltpu.VMEM((NZ, HD, HD), BF),
            pltpu.VMEM((NZ, HD, HD), BF),
            pltpu.VMEM((HALF, HD, HD), BF),
            pltpu.VMEM((HALF, HD, HD), BF),
            pltpu.VMEM((HALF, HD, HD), BF),
            pltpu.VMEM((TOK, HD), F32),
            pltpu.VMEM((4, TOK, HD), F32),
            pltpu.SMEM((2 * UNITS,), jnp.int32),
            pltpu.SemaphoreType.DMA((5,)),
            pltpu.SemaphoreType.DMA((4,)),
            pltpu.SemaphoreType.DMA((len(PART_SIZES) * 2 * UNITS,)),
            pltpu.SemaphoreType.DMA((n_sends,)),
            pltpu.SemaphoreType.DMA((len(PART_SIZES) * UNITS,)),
            pltpu.SemaphoreType.DMA((28,)),
            pltpu.SemaphoreType.DMA((28,)),
        ],
        compiler_params=pltpu.CompilerParams(
            collective_id=0, has_side_effects=True, vmem_limit_bytes=62 * 2**20
        ),
    )(
        q_lin, k_lin, v_lin, gate, queries, keys, values, log_decay, norm_gain.reshape(1, WIDTH), order
    )
    return pl.pallas_call(
        hand_over,
        out_shape=(out, out),
        in_specs=[hbm, hbm],
        out_specs=(hbm, hbm),
        scratch_shapes=[
            pltpu.VMEM((2, TOK, WIDTH), BF), pltpu.SemaphoreType.DMA((4,)), pltpu.SemaphoreType.DMA((4,))
        ],
        compiler_params=pltpu.CompilerParams(vmem_limit_bytes=4 * 2**20),
    )(mixed, attended)


def solution(mesh):
    finer = Mesh(
        mesh.devices.reshape(NY, NZ, 2, mesh.shape["head"]), ("y", "z", "c", "x")
    )
    rows = ("y", "z", "c")
    tile = P(rows, "x")
    return jax.shard_map(
        body,
        mesh=finer,
        in_specs=(tile, tile, tile, P("x", rows), tile, P("x"), tile, tile, tile, P(rows)),
        out_specs=(tile, tile),
        check_vma=False,
    )
```
